256 devices in a mesh: emit: 8 (over y, z_hi), client: 32 (over x, z_lo, core).
Axes of the slice: x: 4, y: 4, z: 8 (z_hi: 2, z_lo: 4; z = z_hi * 4 + z_lo), core: 2. Of those that a mesh axis runs over, the one named last changes fastest.
Arguments:
- features: bfloat16 [131072, 768], P('client'), may hold values from -28 to 28
- labels: int32 [131072], P('client'), may hold values from 0 to 999
- client_ids: int32 [256], replicated, may hold values from 0 to 255, each once
- trunk_in: bfloat16 [256, 2048], replicated, may hold values from -6 to 6
- trunk_weight: bfloat16 [2048, 2048], P(None, 'client'), may hold values from -0.125 to 0.125
- class_table: bfloat16 [1000, 2048], P('emit'), may hold values from -6 to 6
- emit_weight: bfloat16 [2048, 768], P('emit'), may hold values from -0.125 to 0.125
Outputs:
- loss: float32 [131072], P('client')
- emit_grad: float32 [2048, 768], P(('emit', 'client'))
- trunk_grad: float32 [2048, 2048], P(None, ('emit', 'client'))
The draws below stay inside these ranges and needn't reach their ends.
Inputs may be any that keep to these rules, and one draw needn't show every extreme that they name: Each client number appears once; slot s holds the features of client client_ids[s].
All inputs are finite; a program needn't handle non-finite values.
Results may differ from the reference program's by a relative error of at most 0.022.
Values may be sent and summed in bfloat16 or wider, within the bound.
A program may use at most 128 MiB of HBM per device.

```python
import jax
import jax.numpy as jnp
from jax import lax

FEAT = 768
HYPER = 2048
CLASSES = 1000
SAMPLES = 512
CLIENTS = 256


def draw_features(key, part):
    key_base = jax.random.fold_in(key, 11)
    base = jnp.clip(jax.random.normal(key_base, (CLIENTS * SAMPLES, FEAT), jnp.float32), -6.0, 6.0)
    return base.astype(jnp.bfloat16)


def set_ends(array, key, smallest, high):
    spot = [jax.random.randint(jax.random.fold_in(key, axis), (), 0, length) for axis, length in enumerate(array.shape)]
    main_axis = array.shape.index(max(array.shape))
    neighbour = spot[:main_axis] + [(spot[main_axis] + 1) % array.shape[main_axis]] + spot[main_axis + 1:]
    return array.at[tuple(spot)].set(smallest).at[tuple(neighbour)].set(high)


def block_scale(stream_key, dims, split, smallest, high):
    def one(axis_at, blocks):
        steps = jax.random.uniform(jax.random.fold_in(jax.random.fold_in(stream_key, 6), axis_at), (blocks,), jnp.float32, smallest / len(split), high / len(split))
        return jnp.repeat(jnp.exp(steps), dims[axis_at] // blocks).reshape((-1,) + (1,) * (len(dims) - axis_at - 1))

    level = one(*split[0])
    for cut in split[1:]:
        level = level * one(*cut)
    return level


def centred(stream_key, extent, deviation, reach, split=(), held_as=jnp.bfloat16):
    values = deviation * jax.random.normal(stream_key, extent, jnp.float32)
    if split:
        values = values * block_scale(stream_key, extent, split, -0.22, 0.18)
    return jnp.clip(values, -reach, reach).astype(held_as)


def setup_inputs(seed: int = 0) -> dict:
    seeds = jax.random.split(jax.random.key(seed), 8)
    features = draw_features(jax.random.fold_in(seeds[7], 71), 0)
    labels = set_ends(jax.random.randint(seeds[1], (CLIENTS * SAMPLES,), 0, CLASSES), jax.random.fold_in(seeds[1], 1), 0, CLASSES - 1).astype(jnp.int32)
    client_ids = jax.random.permutation(seeds[2], CLIENTS).astype(jnp.int32)
    trunk_in = centred(seeds[3], (CLIENTS, HYPER), 1.0, 6.0)
    trunk_weight = centred(seeds[4], (HYPER, HYPER), HYPER ** -0.5, 0.125, ((1, 32),))
    class_table = centred(seeds[5], (CLASSES, HYPER), 1.0, 6.0, ((0, 8),))
    emit_weight = centred(seeds[6], (HYPER, FEAT), HYPER ** -0.5, 0.125, ((0, 8),))
    return {"features": features, "labels": labels, "client_ids": client_ids, "trunk_in": trunk_in, "trunk_weight": trunk_weight, "class_table": class_table, "emit_weight": emit_weight}


def silu_grad(value):
    sig = jax.nn.sigmoid(value)
    return sig * (1.0 + value * (1.0 - sig))

def reference(features, labels, client_ids, trunk_in, trunk_weight, class_table, emit_weight):
    pre = jnp.dot(trunk_in, trunk_weight, preferred_element_type=jnp.float32).astype(jnp.bfloat16)
    pre_slots = pre[client_ids.astype(jnp.int32)].astype(jnp.float32)
    feats = features.reshape(CLIENTS, SAMPLES, FEAT)
    labs = labels.reshape(CLIENTS, SAMPLES)
    table = class_table.astype(jnp.float32)
    classes = jnp.arange(CLASSES, dtype=jnp.int32)

    def per_slot(carry, item):
        pre_row, feat, lab = item
        code_in = jax.nn.silu(pre_row)[None, :] + table
        code = jax.nn.silu(code_in).astype(jnp.bfloat16)
        heads = jnp.dot(code, emit_weight, preferred_element_type=jnp.float32).astype(jnp.bfloat16)
        logits = jnp.dot(feat, heads.T, preferred_element_type=jnp.float32)
        top = lax.optimization_barrier(jnp.max(logits, axis=1, keepdims=True))
        expd = jnp.exp(logits - top)
        total = lax.optimization_barrier(jnp.sum(expd, axis=1, keepdims=True))
        onehot = (lab[:, None] == classes[None, :]).astype(jnp.float32)
        loss = top[:, 0] + jnp.log(total[:, 0]) - lax.optimization_barrier(jnp.sum(logits * onehot, axis=1))
        grad_logits = ((expd / total - onehot) / CLIENTS).astype(jnp.bfloat16)
        grad_heads = jnp.dot(grad_logits.T, feat, preferred_element_type=jnp.float32).astype(jnp.bfloat16)
        carry = carry + jnp.dot(code.T, grad_heads, preferred_element_type=jnp.float32)
        grad_code = jnp.dot(grad_heads, emit_weight.T, preferred_element_type=jnp.float32)
        grad_sum = lax.optimization_barrier(jnp.sum(grad_code * silu_grad(code_in), axis=0))
        grad_pre = (grad_sum * silu_grad(pre_row)).astype(jnp.bfloat16)
        return (carry, (loss, grad_pre))
    emit_grad, (loss, grad_pre) = lax.scan(per_slot, jnp.zeros((HYPER, FEAT), jnp.float32), (pre_slots, feats, labs))
    grad_client = jnp.zeros((CLIENTS, HYPER), jnp.bfloat16).at[client_ids.astype(jnp.int32)].set(grad_pre)
    trunk_grad = jnp.dot(trunk_in.T, grad_client, preferred_element_type=jnp.float32)
    return (loss.reshape(CLIENTS * SAMPLES), emit_grad, trunk_grad)
```

```python
import jax
import jax.numpy as jnp
from jax import lax
from jax.experimental import pallas as pl
from jax.experimental.pallas import tpu as pltpu
from jax.sharding import PartitionSpec as P

MESH = pl.DeviceIdType.MESH
BF16 = jnp.bfloat16
F32 = jnp.float32

NY, NZH, NX, NZL, NK = 4, 2, 4, 4, 2
NE, NC = NY * NZH, NX * NZL * NK
SLOTS = 8
SAMPLES = 512
CPAD = 128
ROWS = SLOTS * CPAD
HID = 2048
FEAT = 768
CLIENTS = 256
HB = HID // NE
QR = HB // NX


def dot(a, b):
    return jnp.dot(a, b, preferred_element_type=F32)


def dot_nt(a, b):
    return lax.dot_general(a, b, (((1,), (1,)), ((), ())), preferred_element_type=F32)


def dot_tn(a, b):
    return lax.dot_general(a, b, (((0,), (0,)), ((), ())), preferred_element_type=F32)


def sigmoid(v):
    return 0.5 * jnp.tanh(0.5 * v) + 0.5


def step_kernel(
    feats_hbm, labels_ref, ids_ref, trunk_hbm, tw_hbm, table_hbm, emit_hbm,
    loss_ref, egrad_ref, tgrad_ref,
    feats, trunk, tw, table, tablef, wfull,
    pre_send, pre_recv, pre_own, spre, dpre,
    code, code_t, dcode, heads, probs, tops,
    st_send, st_recv, res_send, res_recv,
    gh, eg, egr, am, rx, ry, bx, rxy, by, ryx, cz, rz,
    gs_send, gs_recv, gp_send, gp_recv, trunk_perm,
    loc_sem, pre_ssem, pre_rsem,
    wa_s, wa_r, wz_s, wz_r, wb_s, wb_r, wc_s, wc_r, wd_s, wd_r,
    st_s, st_r, res_s, res_r, core_s, core_r,
    x1_s, x1_r, y1_s, y1_r, x2_s, x2_r, y2_s, y2_r, z_s, z_r,
    gs_s, gs_r, gp_ssem, gp_rsem,
):
    e = lax.axis_index("emit")
    c = lax.axis_index("client")
    y, zh = e // NZH, e % NZH
    x, zl, core = c // (NZL * NK), (c // NK) % NZL, c % NK
    z = zh * NZL + zl
    classes = table_hbm.shape[0]

    def dev(y_=None, z_=None, x_=None, core_=None):
        y_ = y if y_ is None else y_
        z_ = z if z_ is None else z_
        x_ = x if x_ is None else x_
        core_ = core if core_ is None else core_
        return {"emit": y_ * NZH + z_ // NZL, "client": (x_ * NZL + z_ % NZL) * NK + core_}

    def remote(src, dst, ssem, rsem, to):
        return pltpu.make_async_remote_copy(
            src_ref=src, dst_ref=dst, send_sem=ssem, recv_sem=rsem, device_id=to, device_id_type=MESH
        )

    own_w = wfull.at[y, zh]
    ld_trunk = pltpu.make_async_copy(trunk_hbm, trunk, loc_sem.at[0])
    ld_tw = pltpu.make_async_copy(tw_hbm, tw, loc_sem.at[1])
    ld_w = pltpu.make_async_copy(emit_hbm, own_w, loc_sem.at[2])
    ld_table = pltpu.make_async_copy(table_hbm, table, loc_sem.at[3])
    ld_feats = pltpu.make_async_copy(feats_hbm, feats, loc_sem.at[4])
    for cp in (ld_w, ld_trunk, ld_tw, ld_table, ld_feats):
        cp.start()

    ld_w.wait()
    qrow = x * QR + core * (QR // NK)
    qpart = pl.ds(pl.multiple_of(qrow, QR // NK), QR // NK)
    hpart = pl.ds(pl.multiple_of(core * (HB // NK), HB // NK), HB // NK)
    w_z = remote(wfull.at[y, zh, qpart], wfull.at[y, zh, qpart], wz_s, wz_r, dev(z_=2 * NZL - 1 - z))
    w_z.start()
    w_a = []
    for d in range(1, NY):
        part = wfull.at[y, zh, hpart]
        cp = remote(part, part, wa_s.at[d - 1], wa_r.at[d - 1], dev(y_=(y + d) % NY))
        cp.start()
        w_a.append(cp)

    ld_trunk.wait()
    ld_tw.wait()
    cols = dot_nt(trunk[...], tw[...]).astype(BF16)
    width = cols.shape[1]
    spread = (
        lax.broadcasted_iota(jnp.int32, (width, NK * width), 1)
        == lax.broadcasted_iota(jnp.int32, (width, NK * width), 0) + core * width
    ).astype(BF16)
    cols = dot(cols, spread).astype(BF16)
    picker = (
        lax.broadcasted_iota(jnp.int32, (CLIENTS, CLIENTS), 0) == ids_ref[...]
    ).astype(BF16)
    pre_send[...] = dot_tn(picker, cols).reshape(NC, SLOTS, NK * width)

    def send_pre(d, carry):
        to = (c + d) % NC
        remote(pre_send.at[to], pre_recv.at[c], pre_ssem, pre_rsem, {"client": to}).start()
        return carry

    lax.fori_loop(1, NC, send_pre, 0)
    own_pre = pltpu.make_async_copy(pre_send.at[c], pre_recv.at[c], pre_rsem)
    own_pre.start()

    w_z.wait()
    w_b = []
    for d in range(1, NY):
        part = wfull.at[y, 1 - zh, qpart]
        cp = remote(part, part, wb_s.at[d - 1], wb_r.at[d - 1], dev(y_=(y + d) % NY))
        cp.start()
        w_b.append(cp)

    trunk_perm[...] = dot_tn(picker, trunk[...]).astype(BF16)
    ld_table.wait()
    tablef[...] = jnp.zeros_like(tablef)
    tablef[0:classes, :] = table[...].astype(F32)

    for cp in w_b:
        cp.wait()
    w_c = []
    for d in range(1, NX):
        part = wfull.at[:, 1 - zh, qpart]
        cp = remote(part, part, wc_s.at[d - 1], wc_r.at[d - 1], dev(x_=(x + d) % NX))
        cp.start()
        w_c.append(cp)

    pltpu.make_async_copy(pre_recv, pre_recv, pre_rsem).wait()
    for j in range(HID // CPAD):
        pre_own[:, j * CPAD : (j + 1) * CPAD] = pre_recv[NK * j] + pre_recv[NK * j + 1]
    pre = pre_own[...]
    sig = sigmoid(pre)
    spre[...] = pre * sig
    dp = sig * (1.0 + pre * (1.0 - sig))
    for j in range(NE):
        dpre[j] = dp[:, j * HB : (j + 1) * HB]

    live = lax.broadcasted_iota(jnp.int32, (CPAD, HB), 0) < classes

    def emit_codes(first, last):
        def one(i, carry):
            s, h = i // NE, i % NE
            lanes = pl.ds(pl.multiple_of(h * HB, HB), HB)
            rows = pl.ds(pl.multiple_of(s * CPAD, CPAD), CPAD)
            v = spre[pl.ds(s, 1), lanes] + tablef[:, lanes]
            g = sigmoid(v)
            a = v * g
            code[rows, lanes] = jnp.where(live, a, 0.0).astype(BF16)
            dcode[rows, lanes] = (g + a * (1.0 - g)).astype(BF16)
            return carry

        lax.fori_loop(first * NE, last * NE, one, 0)

    emit_codes(0, 4)
    w_d = []
    for i, cp in enumerate(w_a):
        cp.wait()
        part = wfull.at[(y + NY - 1 - i) % NY, zh, hpart]
        cp = remote(part, part, wd_s.at[i], wd_r.at[i], dev(core_=1 - core))
        cp.start()
        w_d.append(cp)
    emit_codes(4, 8)
    for cp in w_c:
        cp.wait()
    for q in range(NX):
        part = wfull.at[:, 1 - zh, pl.ds(pl.multiple_of(q * QR + core * (QR // NK), QR // NK), QR // NK)]
        cp = remote(part, part, wd_s.at[3 + q], wd_r.at[3 + q], dev(core_=1 - core))
        cp.start()
        w_d.append(cp)
    for cp in w_d:
        cp.wait()

    def make_heads(m, carry):
        rows = pl.ds(pl.multiple_of(m * HB, HB), HB)
        heads[rows, :] = dot(code[rows, :], wfull[...].reshape(HID, FEAT)).astype(BF16)
        return carry

    lax.fori_loop(0, ROWS // HB, make_heads, 0)
    ld_feats.wait()

    kids = lax.broadcasted_iota(jnp.int32, (CPAD, SAMPLES), 0)
    valid = kids < classes
    kids = kids + e * classes

    def onehot_of(s):
        return jnp.logical_and(kids == labels_ref[pl.ds(s, 1), :], valid)

    def logits_of(s, carry):
        rows = pl.ds(pl.multiple_of(s * CPAD, CPAD), CPAD)
        frows = pl.ds(pl.multiple_of(s * SAMPLES, SAMPLES), SAMPLES)
        lg = dot_nt(heads[rows, :], feats[frows, :])
        top = jnp.max(jnp.where(valid, lg, -jnp.inf), axis=0, keepdims=True)
        ex = jnp.where(valid, jnp.exp(lg - top), 0.0)
        probs[rows, :] = ex
        tops[pl.ds(s, 1), :] = top
        st_send[s, 0:1, :] = top
        st_send[s, 1:2, :] = jnp.sum(ex, axis=0, keepdims=True)
        st_send[s, 2:3, :] = jnp.sum(jnp.where(onehot_of(s), lg, 0.0), axis=0, keepdims=True)
        st_send[s, 3:4, :] = top
        return carry

    lax.fori_loop(0, SLOTS, logits_of, 0)

    st = []
    for d in range(1, NE):
        to = (e + d) % NE
        cp = remote(st_send.at[to], st_recv.at[d - 1], st_s.at[d - 1], st_r.at[d - 1], {"emit": to})
        cp.start()
        st.append(cp)

    def turn(i, carry):
        s, h = i // NE, i % NE
        rows = pl.ds(pl.multiple_of(s * CPAD, CPAD), CPAD)
        lanes = pl.ds(pl.multiple_of(h * HB, HB), HB)
        code_t[h, :, rows] = code[rows, lanes].T
        return carry

    lax.fori_loop(0, SLOTS * NE // 2, turn, 0)

    for cp in st:
        cp.wait()
    own_st = st_send[e]
    every = [own_st] + [st_recv[d] for d in range(NE - 1)]
    gtop = every[0][0:1]
    for it in every[1:]:
        gtop = jnp.maximum(gtop, it[0:1])
    total = jnp.zeros_like(gtop)
    target = jnp.zeros_like(gtop)
    for it in every:
        total += it[1:2] * jnp.exp(it[0:1] - gtop)
        target += it[2:3]
    logz = gtop + jnp.log(total)
    res_send[0:1, :] = logz
    res_send[1:2, :] = logz - target
    rs = []
    for d in range(1, NE):
        cp = remote(res_send, res_recv.at[e], res_s.at[d - 1], res_r.at[d - 1], {"emit": (e + d) % NE})
        cp.start()
        rs.append(cp)
    res_recv[e] = res_send[...]
    lax.fori_loop(SLOTS * NE // 2, SLOTS * NE, turn, 0)
    for cp in rs:
        cp.wait()

    def grads_of(s, carry):
        rows = pl.ds(pl.multiple_of(s * CPAD, CPAD), CPAD)
        frows = pl.ds(pl.multiple_of(s * SAMPLES, SAMPLES), SAMPLES)
        scale = jnp.exp(tops[pl.ds(s, 1), :] - res_recv[s, 0:1, :])
        g = probs[rows, :] * scale - onehot_of(s).astype(F32)
        gh[rows, :] = dot((g * (1.0 / CLIENTS)).astype(BF16), feats[frows, :]).astype(BF16)
        loss_ref[pl.ds(s, 1), :] = res_recv[s, 1:2, :]
        return carry

    lax.fori_loop(0, SLOTS, grads_of, 0)

    def core_copy(n):
        return remote(eg.at[n, 1 - core], egr.at[n], core_s.at[n], core_r.at[n], dev(core_=1 - core))

    def x1_copy(i, d):
        to = (x + d) % NX
        part = pl.ds(pl.multiple_of(to * 32, 32), 32)
        return remote(am.at[2 * i, part], rx.at[i, d - 1], x1_s.at[i, d - 1], x1_r.at[i, d - 1], dev(x_=to))

    def y1_copy(i):
        return remote(am.at[2 * i + 1], ry.at[i], y1_s.at[i], y1_r.at[i], dev(y_=(y + 1 + i) % NY))

    def compute_chunk(i):
        yy = (y + 1 + i) % NY
        for half in range(NZH):
            n = 2 * i + half
            part = dot(code_t[yy * NZH + half], gh[...]).reshape(16, NK, 8, FEAT)
            for k in range(NK):
                eg[n, k] = part[:, k].reshape(HB // NK, FEAT).astype(BF16)
            core_copy(n).start()

    def pass_on(i, last):
        for half in range(NZH):
            n = 2 * i + half
            core_copy(n).wait()
            am[n] = (eg[n, core].astype(F32) + egr[n].astype(F32)).astype(BF16)
            if half == 0:
                for d in range(1, NX):
                    x1_copy(i, d).start()
            elif not last:
                y1_copy(i).start()

    compute_chunk(0)

    def chunk_step(i, carry):
        compute_chunk(i)
        pass_on(i - 1, False)
        return carry

    lax.fori_loop(1, NY, chunk_step, 0)

    def sum_codes(h, carry):
        gc = dot_nt(gh[...], wfull[h // NZH, h % NZH])
        for s in range(SLOTS):
            lanes = pl.ds(pl.multiple_of(h * HB, HB), HB)
            part = gc[s * CPAD : (s + 1) * CPAD] * dcode[s * CPAD : (s + 1) * CPAD, lanes].astype(F32)
            gs_send[h, s : s + 1, :] = jnp.sum(part, axis=0, keepdims=True)
        return carry

    lax.fori_loop(0, 1, sum_codes, 0)
    pass_on(NY - 1, True)
    lax.fori_loop(1, NE, sum_codes, 0)

    gs = []
    for d in range(1, NE):
        to = (e + d) % NE
        cp = remote(gs_send.at[to], gs_recv.at[d - 1], gs_s.at[d - 1], gs_r.at[d - 1], {"emit": to})
        cp.start()
        gs.append(cp)

    xpart = pl.ds(pl.multiple_of(x * 32, 32), 32)
    y2 = []
    for i in range(NY):
        for d in range(1, NX):
            x1_copy(i, d).wait()
        acc = am[2 * i, xpart, :].astype(F32)
        for d in range(NX - 1):
            acc += rx[i, d].astype(F32)
        bx[i] = acc.astype(BF16)
        if i < NY - 1:
            cp = remote(bx.at[i], rxy.at[i], y2_s.at[i], y2_r.at[i], dev(y_=(y + 1 + i) % NY))
            cp.start()
            y2.append(cp)
    acc = am[2 * NY - 1].astype(F32)
    for i in range(NY - 1):
        y1_copy(i).wait()
        acc += ry[i].astype(F32)
    by[...] = acc.astype(BF16)
    x2 = []
    for d in range(1, NX):
        to = (x + d) % NX
        part = pl.ds(pl.multiple_of(to * 32, 32), 32)
        cp = remote(by.at[part], ryx.at[d - 1], x2_s.at[d - 1], x2_r.at[d - 1], dev(x_=to))
        cp.start()
        x2.append(cp)

    for cp in gs:
        cp.wait()
    block = gs_send[e]
    for d in range(NE - 1):
        block = block + gs_recv[d]
    gp_send[...] = (block * dpre[e]).astype(BF16)

    def send_gp(d, carry):
        remote(gp_send, gp_recv.at[c], gp_ssem, gp_rsem, {"client": (c + d) % NC}).start()
        return carry

    lax.fori_loop(1, NC, send_gp, 0)
    own_gp = pltpu.make_async_copy(gp_send, gp_recv.at[c], gp_rsem)
    own_gp.start()

    for cp in y2:
        cp.wait()
    acc = bx[NY - 1].astype(F32)
    for d in range(NY - 1):
        acc += rxy[d].astype(F32)
    cz[0:NZL] = acc.astype(BF16).reshape(NZL, 8, FEAT)
    for cp in x2:
        cp.wait()
    acc = by[xpart, :].astype(F32)
    for d in range(NX - 1):
        acc += ryx[d].astype(F32)
    cz[NZL:] = acc.astype(BF16).reshape(NZL, 8, FEAT)
    nz = NZH * NZL
    zs = []
    for d in range(1, nz):
        to = (z + d) % nz
        cp = remote(cz.at[to], rz.at[d - 1], z_s.at[d - 1], z_r.at[d - 1], dev(z_=to))
        cp.start()
        zs.append(cp)

    pltpu.make_async_copy(gp_recv, gp_recv, gp_rsem).wait()
    select = (
        lax.broadcasted_iota(jnp.int32, (8, HB), 1) == lax.broadcasted_iota(jnp.int32, (8, HB), 0) + c * 8
    ).astype(BF16)
    mine = dot_nt(select, gp_recv[...].reshape(CLIENTS, HB)).astype(BF16)
    tgrad_ref[...] = dot(mine, trunk_perm[...])

    for cp in zs:
        cp.wait()
    acc = cz[z].astype(F32)
    for d in range(nz - 1):
        acc += rz[d].astype(F32)
    egrad_ref[...] = acc

    remote(pre_send.at[0 : NC - 1], pre_recv.at[0 : NC - 1], pre_ssem, pre_rsem, {"client": (c + 1) % NC}).wait_send()
    remote(gp_recv.at[0 : NC - 1], gp_recv.at[0 : NC - 1], gp_ssem, gp_rsem, {"client": (c + 1) % NC}).wait_send()


def per_device(features, labels, client_ids, trunk_in, trunk_weight, class_table, emit_weight):
    vm = pltpu.VMEM
    dma = pltpu.SemaphoreType.DMA
    half = HB // NK
    scratch = [
        vm((SLOTS * SAMPLES, FEAT), BF16), vm((CLIENTS, HID), BF16), vm((trunk_weight.shape[1], HID), BF16),
        vm(class_table.shape, BF16), vm((CPAD, HID), F32), vm((NY, NZH, HB, FEAT), BF16),
        vm((NC, SLOTS, CPAD), F32), vm((NC, SLOTS, CPAD), F32), vm((SLOTS, HID), F32), vm((SLOTS, HID), F32),
        vm((NE, SLOTS, HB), F32),
        vm((ROWS, HID), BF16), vm((NE, HB, ROWS), BF16), vm((ROWS, HID), BF16), vm((ROWS, FEAT), BF16),
        vm((ROWS, SAMPLES), F32), vm((SLOTS, SAMPLES), F32),
        vm((SLOTS, 4, SAMPLES), F32), vm((NE - 1, 4, SAMPLES), F32), vm((2, SAMPLES), F32), vm((SLOTS, 2, SAMPLES), F32),
        vm((ROWS, FEAT), BF16), vm((NE, NK, half, FEAT), BF16), vm((NE, half, FEAT), BF16), vm((NE, half, FEAT), BF16),
        vm((NY, NX - 1, 32, FEAT), BF16), vm((NY - 1, half, FEAT), BF16),
        vm((NY, 32, FEAT), BF16), vm((NY - 1, 32, FEAT), BF16), vm((half, FEAT), BF16), vm((NX - 1, 32, FEAT), BF16),
        vm((NZH * NZL, 8, FEAT), BF16), vm((NZH * NZL - 1, 8, FEAT), BF16),
        vm((NE, SLOTS, HB), F32), vm((NE - 1, SLOTS, HB), F32), vm((SLOTS, HB), BF16), vm((NC, SLOTS, HB), BF16),
        vm((CLIENTS, HID), BF16),
        dma((5,)), dma, dma,
        dma((3,)), dma((3,)), dma, dma, dma((3,)), dma((3,)), dma((3,)), dma((3,)), dma((7,)), dma((7,)),
        dma((7,)), dma((7,)), dma((7,)), dma((7,)), dma((8,)), dma((8,)),
        dma((4, 3)), dma((4, 3)), dma((3,)), dma((3,)), dma((3,)), dma((3,)), dma((3,)), dma((3,)), dma((7,)), dma((7,)),
        dma((7,)), dma((7,)), dma, dma,
    ]
    hbm = pl.BlockSpec(memory_space=pl.ANY)
    here = pl.BlockSpec(memory_space=pltpu.VMEM)
    loss, egrad, tgrad = pl.pallas_call(
        step_kernel,
        name="hyper_step",
        out_shape=(
            jax.ShapeDtypeStruct((SLOTS, SAMPLES), F32),
            jax.ShapeDtypeStruct((HID // (NE * NC), FEAT), F32),
            jax.ShapeDtypeStruct((HID // (NE * NC), HID), F32),
        ),
        in_specs=[hbm, here, here, hbm, hbm, hbm, hbm],
        out_specs=(here, here, here),
        scratch_shapes=scratch,
        compiler_params=pltpu.CompilerParams(has_side_effects=True, vmem_limit_bytes=56 << 20),
    )(
        features, labels.reshape(SLOTS, SAMPLES), client_ids.reshape(1, CLIENTS), trunk_in, trunk_weight.T,
        class_table, emit_weight,
    )
    return loss.reshape(SLOTS * SAMPLES), egrad, tgrad.T


def solution(mesh):
    return jax.shard_map(
        per_device,
        mesh=mesh,
        in_specs=(
            P("client", None),
            P("client"),
            P(),
            P(),
            P(None, "client"),
            P("emit", None),
            P("emit", None),
        ),
        out_specs=(P("client"), P(("emit", "client"), None), P(None, ("emit", "client"))),
        check_vma=False,
    )
```

```python
import jax
import jax.numpy as jnp
from jax import lax
from jax.experimental import pallas as pl
from jax.experimental.pallas import tpu as pltpu
from jax.sharding import PartitionSpec as P

MESH = pl.DeviceIdType.MESH
BF16 = jnp.bfloat16
F32 = jnp.float32

NY, NZH, NX, NZL, NK = 4, 2, 4, 4, 2
NE, NC = NY * NZH, NX * NZL * NK
SLOTS = 8
SAMPLES = 512
CPAD = 128
ROWS = SLOTS * CPAD
HID = 2048
FEAT = 768
CLIENTS = 256
HB = HID // NE
QR = HB // NX


def dot(a, b):
    return jnp.dot(a, b, preferred_element_type=F32)


def dot_nt(a, b):
    return lax.dot_general(a, b, (((1,), (1,)), ((), ())), preferred_element_type=F32)


def dot_tn(a, b):
    return lax.dot_general(a, b, (((0,), (0,)), ((), ())), preferred_element_type=F32)


def sigmoid(v):
    return 0.5 * jnp.tanh(0.5 * v) + 0.5


def step_kernel(
    feats_hbm, labels_ref, ids_ref, trunk_hbm, tw_hbm, table_hbm, emit_hbm,
    loss_ref, egrad_ref, tgrad_ref,
    feats, lab, trunk, tw, table, tablef, wfull,
    pre_send, pre_recv, pre_own, spre, dpre,
    code, code_t, dcode, hacc, heads, probs, tops,
    st_send, st_recv, res_send, res_recv,
    gh, eg, egr, am, rx, ry, bx, rxy, by, ryx, cz, rz,
    gs_send, gs_recv, gp_send, gp_recv, trunk_perm,
    loc_sem, pre_ssem, pre_rsem,
    wa_s, wa_r, wz_s, wz_r, wb_s, wb_r, wc_s, wc_r, wd_s, wd_r,
    st_s, st_r, res_s, res_r, core_s, core_r,
    x1_s, x1_r, y1_s, y1_r, x2_s, x2_r, y2_s, y2_r, z_s, z_r,
    gs_s, gs_r, gp_ssem, gp_rsem,
):
    e = lax.axis_index("emit")
    c = lax.axis_index("client")
    y, zh = e // NZH, e % NZH
    x, zl, core = c // (NZL * NK), (c // NK) % NZL, c % NK
    z = zh * NZL + zl
    classes = table_hbm.shape[0]

    def dev(y_=None, z_=None, x_=None, core_=None):
        y_ = y if y_ is None else y_
        z_ = z if z_ is None else z_
        x_ = x if x_ is None else x_
        core_ = core if core_ is None else core_
        return {"emit": y_ * NZH + z_ // NZL, "client": (x_ * NZL + z_ % NZL) * NK + core_}

    def remote(src, dst, ssem, rsem, to):
        return pltpu.make_async_remote_copy(
            src_ref=src, dst_ref=dst, send_sem=ssem, recv_sem=rsem, device_id=to, device_id_type=MESH
        )

    barrier = pltpu.get_barrier_semaphore()

    def greet(to):
        pl.semaphore_signal(barrier, inc=1, device_id=to, device_id_type=MESH)

    def greet_client(d, carry):
        greet({"client": (c + d) % NC})
        return carry

    for d in range(1, NE):
        greet({"emit": (e + d) % NE})
    for d in range(1, NZL):
        greet(dev(z_=(1 - zh) * NZL + (zl + d) % NZL))
    lax.fori_loop(1, NC, greet_client, 0)

    ld_trunk = pltpu.make_async_copy(trunk_hbm, trunk, loc_sem.at[0])
    ld_tw = pltpu.make_async_copy(tw_hbm, tw, loc_sem.at[1])
    ld_w = pltpu.make_async_copy(emit_hbm, wfull.at[zh, y], loc_sem.at[2])
    ld_table = pltpu.make_async_copy(table_hbm, table, loc_sem.at[3])
    ld_feats = pltpu.make_async_copy(feats_hbm, feats, loc_sem.at[4])
    for cp in (ld_trunk, ld_tw, ld_w, ld_table, ld_feats):
        cp.start()

    ld_trunk.wait()
    ld_tw.wait()
    cols = dot_nt(trunk[...], tw[...]).astype(BF16)
    width = cols.shape[1]
    spread = (
        lax.broadcasted_iota(jnp.int32, (width, NK * width), 1)
        == lax.broadcasted_iota(jnp.int32, (width, NK * width), 0) + core * width
    ).astype(BF16)
    cols = dot(cols, spread).astype(BF16)
    picker = (
        lax.broadcasted_iota(jnp.int32, (CLIENTS, CLIENTS), 0) == ids_ref[...]
    ).astype(BF16)
    pre_send[...] = dot_tn(picker, cols).reshape(NC, SLOTS, NK * width)
    ld_table.wait()
    tablef[...] = jnp.zeros_like(tablef)
    tablef[0:classes, :] = table[...].astype(F32)
    for s in range(SLOTS):
        for j in range(SAMPLES // 128):
            lab[s : s + 1, j * 128 : (j + 1) * 128] = labels_ref[s * 4 + j : s * 4 + j + 1, :]
    ld_w.wait()

    pl.semaphore_wait(barrier, NE - 1 + NZL - 1 + NC - 1)

    qrow = x * QR + core * (QR // NK)
    qpart = pl.ds(pl.multiple_of(qrow, QR // NK), QR // NK)
    half = HB // NK
    cut = 32

    def hpart(first, last):
        return pl.ds(pl.multiple_of(core * half + first, cut), last - first)

    w_z = remote(wfull.at[zh, y, qpart], wfull.at[zh, y, qpart], wz_s, wz_r, dev(z_=2 * NZL - 1 - z))
    w_z.start()

    def send_pre(d, carry):
        to = (c + d) % NC
        remote(pre_send.at[to], pre_recv.at[c], pre_ssem, pre_rsem, {"client": to}).start()
        return carry

    lax.fori_loop(1, NC, send_pre, 0)
    own_pre = pltpu.make_async_copy(pre_send.at[c], pre_recv.at[c], pre_rsem)
    own_pre.start()
    w_a = []
    for d in range(1, NY):
        part = wfull.at[zh, y, hpart(0, cut)]
        cp = remote(part, part, wa_s.at[0, d - 1], wa_r.at[0, d - 1], dev(y_=(y + d) % NY))
        cp.start()
        w_a.append(cp)

    w_z.wait()
    w_b = []
    for d in range(1, NY):
        part = wfull.at[1 - zh, y, qpart]
        cp = remote(part, part, wb_s.at[d - 1], wb_r.at[d - 1], dev(y_=(y + d) % NY))
        cp.start()
        w_b.append(cp)
    for d in range(1, NY):
        part = wfull.at[zh, y, hpart(cut, half)]
        cp = remote(part, part, wa_s.at[1, d - 1], wa_r.at[1, d - 1], dev(y_=(y + d) % NY))
        cp.start()
        w_a.append(cp)

    pltpu.make_async_copy(pre_recv, pre_recv, pre_rsem).wait()
    for j in range(HID // CPAD):
        pre_own[:, j * CPAD : (j + 1) * CPAD] = pre_recv[NK * j] + pre_recv[NK * j + 1]
    pre = pre_own[...]
    sig = sigmoid(pre)
    spre[...] = pre * sig
    dp = sig * (1.0 + pre * (1.0 - sig))
    for j in range(NE):
        dpre[j] = dp[:, j * HB : (j + 1) * HB]

    live = lax.broadcasted_iota(jnp.int32, (CPAD, HB), 0) < classes

    def emit_codes(i, carry):
        s, h = i // NE, i % NE
        lanes = pl.ds(pl.multiple_of(h * HB, HB), HB)
        within = pl.ds(pl.multiple_of((h // NZH) * HB, HB), HB)
        rows = pl.ds(pl.multiple_of(s * CPAD, CPAD), CPAD)
        v = spre[pl.ds(s, 1), lanes] + tablef[:, lanes]
        g = sigmoid(v)
        a = v * g
        code[h % NZH, rows, within] = jnp.where(live, a, 0.0).astype(BF16)
        dcode[rows, lanes] = (g + a * (1.0 - g)).astype(BF16)
        return carry

    def turn(i, carry):
        s, h = i // NE, i % NE
        rows = pl.ds(pl.multiple_of(s * CPAD, CPAD), CPAD)
        within = pl.ds(pl.multiple_of((h // NZH) * HB, HB), HB)
        code_t[h, :, rows] = code[h % NZH, rows, within].T
        return carry

    lax.fori_loop(0, NE, emit_codes, 0)

    for cp in w_b:
        cp.wait()
    w_c = []
    for d in range(1, NX):
        part = wfull.at[1 - zh, :, qpart]
        cp = remote(part, part, wc_s.at[d - 1], wc_r.at[d - 1], dev(x_=(x + d) % NX))
        cp.start()
        w_c.append(cp)

    def to_core(i, q):
        part = wfull.at[1 - zh, :, pl.ds(pl.multiple_of(q * QR + core * (QR // NK), QR // NK), QR // NK)]
        return remote(part, part, wd_s.at[i], wd_r.at[i], dev(core_=1 - core))

    w_d = [to_core(3, x)]
    w_d[0].start()

    lax.fori_loop(NE, SLOTS * NE, emit_codes, 0)
    lax.fori_loop(0, SLOTS * NE // 2, turn, 0)
    trunk_perm[...] = dot_tn(picker, trunk[...]).astype(BF16)

    w_e = []
    for d in range(1, NY):
        w_a[d - 1].wait()
        w_a[NY - 1 + d - 1].wait()
        part = wfull.at[zh, (y + NY - d) % NY, hpart(0, half)]
        cp = remote(part, part, wd_s.at[d - 1], wd_r.at[d - 1], dev(core_=1 - core))
        cp.start()
        w_e.append(cp)
    lax.fori_loop(SLOTS * NE // 2, SLOTS * NE, turn, 0)
    for cp in w_e:
        cp.wait()

    def heads_first(m, carry):
        rows = pl.ds(pl.multiple_of(m * HB, HB), HB)
        hacc[rows, :] = dot(code[zh, rows, :], wfull[zh].reshape(HID // NZH, FEAT))
        return carry

    lax.fori_loop(0, ROWS // HB, heads_first, 0)

    for d in range(1, NX):
        w_c[d - 1].wait()
        cp = to_core(3 + d, (x + NX - d) % NX)
        cp.start()
        w_d.append(cp)
    for cp in w_d:
        cp.wait()

    def heads_rest(m, carry):
        rows = pl.ds(pl.multiple_of(m * HB, HB), HB)
        part = dot(code[1 - zh, rows, :], wfull[1 - zh].reshape(HID // NZH, FEAT))
        heads[rows, :] = (hacc[rows, :] + part).astype(BF16)
        return carry

    lax.fori_loop(0, ROWS // HB, heads_rest, 0)
    ld_feats.wait()

    kids = lax.broadcasted_iota(jnp.int32, (CPAD, SAMPLES), 0)
    valid = kids < classes
    kids = kids + e * classes

    def onehot_of(s):
        return jnp.logical_and(kids == lab[pl.ds(s, 1), :], valid)

    def logits_of(s, carry):
        rows = pl.ds(pl.multiple_of(s * CPAD, CPAD), CPAD)
        frows = pl.ds(pl.multiple_of(s * SAMPLES, SAMPLES), SAMPLES)
        lg = dot_nt(heads[rows, :], feats[frows, :])
        top = jnp.max(jnp.where(valid, lg, -jnp.inf), axis=0, keepdims=True)
        ex = jnp.where(valid, jnp.exp(lg - top), 0.0)
        probs[rows, :] = ex
        tops[pl.ds(s, 1), :] = top
        st_send[s, 0:1, :] = top
        st_send[s, 1:2, :] = jnp.sum(ex, axis=0, keepdims=True)
        st_send[s, 2:3, :] = jnp.sum(jnp.where(onehot_of(s), lg, 0.0), axis=0, keepdims=True)
        st_send[s, 3:4, :] = top
        return carry

    lax.fori_loop(0, SLOTS, logits_of, 0)

    st = []
    for d in range(1, NE):
        to = (e + d) % NE
        cp = remote(st_send.at[to], st_recv.at[d - 1], st_s.at[d - 1], st_r.at[d - 1], {"emit": to})
        cp.start()
        st.append(cp)

    for cp in st:
        cp.wait()
    own_st = st_send[e]
    every = [own_st] + [st_recv[d] for d in range(NE - 1)]
    gtop = every[0][0:1]
    for it in every[1:]:
        gtop = jnp.maximum(gtop, it[0:1])
    total = jnp.zeros_like(gtop)
    target = jnp.zeros_like(gtop)
    for it in every:
        total += it[1:2] * jnp.exp(it[0:1] - gtop)
        target += it[2:3]
    logz = gtop + jnp.log(total)
    res_send[0:1, :] = logz
    res_send[1:2, :] = logz - target
    rs = []
    for d in range(1, NE):
        cp = remote(res_send, res_recv.at[e], res_s.at[d - 1], res_r.at[d - 1], {"emit": (e + d) % NE})
        cp.start()
        rs.append(cp)
    res_recv[e] = res_send[...]
    for cp in rs:
        cp.wait()

    def grads_of(s, carry):
        rows = pl.ds(pl.multiple_of(s * CPAD, CPAD), CPAD)
        frows = pl.ds(pl.multiple_of(s * SAMPLES, SAMPLES), SAMPLES)
        scale = jnp.exp(tops[pl.ds(s, 1), :] - res_recv[s, 0:1, :])
        g = probs[rows, :] * scale - onehot_of(s).astype(F32)
        gh[rows, :] = dot((g * (1.0 / CLIENTS)).astype(BF16), feats[frows, :]).astype(BF16)
        return carry

    lax.fori_loop(0, SLOTS, grads_of, 0)

    for s in range(SLOTS):
        for j in range(SAMPLES // 128):
            loss_ref[s * 4 + j : s * 4 + j + 1, :] = res_recv[s, 1:2, j * 128 : (j + 1) * 128]

    def core_copy(n):
        return remote(eg.at[n, 1 - core], egr.at[n], core_s.at[n], core_r.at[n], dev(core_=1 - core))

    def x1_copy(i, d):
        to = (x + d) % NX
        part = pl.ds(pl.multiple_of(to * 32, 32), 32)
        return remote(am.at[2 * i, part], rx.at[i, d - 1], x1_s.at[i, d - 1], x1_r.at[i, d - 1], dev(x_=to))

    def y1_copy(i):
        return remote(am.at[2 * i + 1], ry.at[i], y1_s.at[i], y1_r.at[i], dev(y_=(y + 1 + i) % NY))

    def compute_chunk(i):
        yy = (y + 1 + i) % NY
        for half in range(NZH):
            n = 2 * i + half
            part = dot(code_t[yy * NZH + half], gh[...]).reshape(16, NK, 8, FEAT)
            for k in range(NK):
                eg[n, k] = part[:, k].reshape(HB // NK, FEAT).astype(BF16)
            core_copy(n).start()

    def pass_on(i, last):
        for half in range(NZH):
            n = 2 * i + half
            core_copy(n).wait()
            am[n] = (eg[n, core].astype(F32) + egr[n].astype(F32)).astype(BF16)
            if half == 0:
                for d in range(1, NX):
                    x1_copy(i, d).start()
            elif not last:
                y1_copy(i).start()

    compute_chunk(0)

    def chunk_step(i, carry):
        compute_chunk(i)
        pass_on(i - 1, False)
        return carry

    lax.fori_loop(1, NY, chunk_step, 0)

    def sum_codes(h, carry):
        gc = dot_nt(gh[...], wfull[h % NZH, h // NZH])
        for s in range(SLOTS):
            lanes = pl.ds(pl.multiple_of(h * HB, HB), HB)
            part = gc[s * CPAD : (s + 1) * CPAD] * dcode[s * CPAD : (s + 1) * CPAD, lanes].astype(F32)
            gs_send[h, s : s + 1, :] = jnp.sum(part, axis=0, keepdims=True)
        return carry

    lax.fori_loop(0, 1, sum_codes, 0)
    pass_on(NY - 1, True)
    lax.fori_loop(1, NE, sum_codes, 0)

    gs = []
    for d in range(1, NE):
        to = (e + d) % NE
        cp = remote(gs_send.at[to], gs_recv.at[d - 1], gs_s.at[d - 1], gs_r.at[d - 1], {"emit": to})
        cp.start()
        gs.append(cp)

    xpart = pl.ds(pl.multiple_of(x * 32, 32), 32)
    y2 = []
    for i in range(NY):
        for d in range(1, NX):
            x1_copy(i, d).wait()
        acc = am[2 * i, xpart, :].astype(F32)
        for d in range(NX - 1):
            acc += rx[i, d].astype(F32)
        bx[i] = acc.astype(BF16)
        if i < NY - 1:
            cp = remote(bx.at[i], rxy.at[i], y2_s.at[i], y2_r.at[i], dev(y_=(y + 1 + i) % NY))
            cp.start()
            y2.append(cp)
    acc = am[2 * NY - 1].astype(F32)
    for i in range(NY - 1):
        y1_copy(i).wait()
        acc += ry[i].astype(F32)
    by[...] = acc.astype(BF16)
    x2 = []
    for d in range(1, NX):
        to = (x + d) % NX
        part = pl.ds(pl.multiple_of(to * 32, 32), 32)
        cp = remote(by.at[part], ryx.at[d - 1], x2_s.at[d - 1], x2_r.at[d - 1], dev(x_=to))
        cp.start()
        x2.append(cp)

    for cp in gs:
        cp.wait()
    block = gs_send[e]
    for d in range(NE - 1):
        block = block + gs_recv[d]
    gp_send[...] = (block * dpre[e]).astype(BF16)

    def send_gp(d, carry):
        remote(gp_send, gp_recv.at[c], gp_ssem, gp_rsem, {"client": (c + d) % NC}).start()
        return carry

    lax.fori_loop(1, NC, send_gp, 0)
    own_gp = pltpu.make_async_copy(gp_send, gp_recv.at[c], gp_rsem)
    own_gp.start()

    for cp in y2:
        cp.wait()
    acc = bx[NY - 1].astype(F32)
    for d in range(NY - 1):
        acc += rxy[d].astype(F32)
    cz[0:NZL] = acc.astype(BF16).reshape(NZL, 8, FEAT)
    for cp in x2:
        cp.wait()
    acc = by[xpart, :].astype(F32)
    for d in range(NX - 1):
        acc += ryx[d].astype(F32)
    cz[NZL:] = acc.astype(BF16).reshape(NZL, 8, FEAT)
    nz = NZH * NZL
    zs = []
    for d in range(1, nz):
        to = (z + d) % nz
        cp = remote(cz.at[to], rz.at[d - 1], z_s.at[d - 1], z_r.at[d - 1], dev(z_=to))
        cp.start()
        zs.append(cp)

    pltpu.make_async_copy(gp_recv, gp_recv, gp_rsem).wait()
    select = (
        lax.broadcasted_iota(jnp.int32, (8, HB), 1) == lax.broadcasted_iota(jnp.int32, (8, HB), 0) + c * 8
    ).astype(BF16)
    mine = dot_nt(select, gp_recv[...].reshape(CLIENTS, HB)).astype(BF16)
    tgrad_ref[...] = dot(mine, trunk_perm[...])

    for cp in zs:
        cp.wait()
    acc = cz[z].astype(F32)
    for d in range(nz - 1):
        acc += rz[d].astype(F32)
    egrad_ref[...] = acc

    remote(pre_send.at[0 : NC - 1], pre_recv.at[0 : NC - 1], pre_ssem, pre_rsem, {"client": (c + 1) % NC}).wait_send()
    remote(gp_recv.at[0 : NC - 1], gp_recv.at[0 : NC - 1], gp_ssem, gp_rsem, {"client": (c + 1) % NC}).wait_send()


def hand_over(loss_in, egrad_in, tgrad_in, loss_ref, egrad_ref, tgrad_ref):
    loss_ref[...] = loss_in[...]
    egrad_ref[...] = egrad_in[...]
    tgrad_ref[...] = tgrad_in[...]


def per_device(features, labels, client_ids, trunk_in, trunk_weight, class_table, emit_weight):
    vm = pltpu.VMEM
    dma = pltpu.SemaphoreType.DMA
    half = HB // NK
    scratch = [
        vm((SLOTS * SAMPLES, FEAT), BF16), vm((SLOTS, SAMPLES), jnp.int32), vm((CLIENTS, HID), BF16), vm((trunk_weight.shape[1], HID), BF16),
        vm(class_table.shape, BF16), vm((CPAD, HID), F32), vm((NZH, NY, HB, FEAT), BF16),
        vm((NC, SLOTS, CPAD), F32), vm((NC, SLOTS, CPAD), F32), vm((SLOTS, HID), F32), vm((SLOTS, HID), F32),
        vm((NE, SLOTS, HB), F32),
        vm((NZH, ROWS, HID // NZH), BF16), vm((NE, HB, ROWS), BF16), vm((ROWS, HID), BF16), vm((ROWS, FEAT), F32),
        vm((ROWS, FEAT), BF16),
        vm((ROWS, SAMPLES), F32), vm((SLOTS, SAMPLES), F32),
        vm((SLOTS, 4, SAMPLES), F32), vm((NE - 1, 4, SAMPLES), F32), vm((2, SAMPLES), F32), vm((SLOTS, 2, SAMPLES), F32),
        vm((ROWS, FEAT), BF16), vm((NE, NK, half, FEAT), BF16), vm((NE, half, FEAT), BF16), vm((NE, half, FEAT), BF16),
        vm((NY, NX - 1, 32, FEAT), BF16), vm((NY - 1, half, FEAT), BF16),
        vm((NY, 32, FEAT), BF16), vm((NY - 1, 32, FEAT), BF16), vm((half, FEAT), BF16), vm((NX - 1, 32, FEAT), BF16),
        vm((NZH * NZL, 8, FEAT), BF16), vm((NZH * NZL - 1, 8, FEAT), BF16),
        vm((NE, SLOTS, HB), F32), vm((NE - 1, SLOTS, HB), F32), vm((SLOTS, HB), BF16), vm((NC, SLOTS, HB), BF16),
        vm((CLIENTS, HID), BF16),
        dma((5,)), dma, dma,
        dma((2, 3)), dma((2, 3)), dma, dma, dma((3,)), dma((3,)), dma((3,)), dma((3,)), dma((7,)), dma((7,)),
        dma((7,)), dma((7,)), dma((7,)), dma((7,)), dma((8,)), dma((8,)),
        dma((4, 3)), dma((4, 3)), dma((3,)), dma((3,)), dma((3,)), dma((3,)), dma((3,)), dma((3,)), dma((7,)), dma((7,)),
        dma((7,)), dma((7,)), dma, dma,
    ]
    hbm = pl.BlockSpec(memory_space=pl.ANY)
    here = pl.BlockSpec(memory_space=pltpu.VMEM)
    loss, egrad, tgrad = pl.pallas_call(
        step_kernel,
        name="hyper_step",
        out_shape=(
            jax.ShapeDtypeStruct((SLOTS * SAMPLES // 128, 128), F32),
            jax.ShapeDtypeStruct((HID // (NE * NC), FEAT), F32),
            jax.ShapeDtypeStruct((HID // (NE * NC), HID), F32),
        ),
        in_specs=[hbm, here, here, hbm, hbm, hbm, hbm],
        out_specs=(here, here, here),
        scratch_shapes=scratch,
        compiler_params=pltpu.CompilerParams(collective_id=0, has_side_effects=True, vmem_limit_bytes=56 << 20),
    )(
        features, labels.reshape(SLOTS * SAMPLES // 128, 128), client_ids.reshape(1, CLIENTS), trunk_in, trunk_weight.T,
        class_table, emit_weight,
    )
    outs = (loss, egrad, tgrad)
    loss, egrad, tgrad = pl.pallas_call(
        hand_over,
        name="hand_over",
        out_shape=tuple(jax.ShapeDtypeStruct(o.shape, o.dtype) for o in outs),
        in_specs=[here] * 3,
        out_specs=(here,) * 3,
    )(*outs)
    return loss.reshape(SLOTS * SAMPLES), egrad, tgrad.T


def solution(mesh):
    return jax.shard_map(
        per_device,
        mesh=mesh,
        in_specs=(
            P("client", None),
            P("client"),
            P(),
            P(),
            P(None, "client"),
            P("emit", None),
            P("emit", None),
        ),
        out_specs=(P("client"), P(("emit", "client"), None), P(None, ("emit", "client"))),
        check_vma=False,
    )
```

```python
import jax
import jax.numpy as jnp
from jax import lax
from jax.experimental import pallas as pl
from jax.experimental.pallas import tpu as pltpu
from jax.sharding import PartitionSpec as P

MESH = pl.DeviceIdType.MESH
BF16 = jnp.bfloat16
F32 = jnp.float32

NY, NZH, NX, NZL, NK = 4, 2, 4, 4, 2
NE, NC = NY * NZH, NX * NZL * NK
SLOTS = 8
SAMPLES = 512
CPAD = 128
ROWS = SLOTS * CPAD
HID = 2048
FEAT = 768
CLIENTS = 256
HB = HID // NE
QR = HB // NX


def dot(a, b):
    return jnp.dot(a, b, preferred_element_type=F32)


def dot_nt(a, b):
    return lax.dot_general(a, b, (((1,), (1,)), ((), ())), preferred_element_type=F32)


def dot_tn(a, b):
    return lax.dot_general(a, b, (((0,), (0,)), ((), ())), preferred_element_type=F32)


def sigmoid(v):
    return 0.5 * jnp.tanh(0.5 * v) + 0.5


def step_kernel(
    feats_hbm, labels_ref, ids_ref, trunk_hbm, tw_hbm, table_hbm, emit_hbm,
    loss_ref, egrad_ref, tgrad_ref,
    feats, lab, trunk, tw, table, tablef, wfull,
    pre_send, pre_recv, pre_own, spre, dpre,
    code, code_t, dcode, hacc, heads, probs, tops,
    sums, logz, st_send, st_recv, tg_send, tg_recv,
    gh, eg, egr, am, rx, ry, bx, rxy, by, ryx, cz, rz,
    gs_send, gs_recv, gp_send, gp_recv, trunk_perm,
    loc_sem, pre_ssem, pre_rsem,
    wa_s, wa_r, wz_s, wz_r, wb_s, wb_r, wc_s, wc_r, wd_s, wd_r,
    st_s, st_r, res_s, res_r, core_s, core_r,
    x1_s, x1_r, y1_s, y1_r, x2_s, x2_r, y2_s, y2_r, z_s, z_r,
    gs_s, gs_r, gp_ssem, gp_rsem,
):
    e = lax.axis_index("emit")
    c = lax.axis_index("client")
    y, zh = e // NZH, e % NZH
    x, zl, core = c // (NZL * NK), (c // NK) % NZL, c % NK
    z = zh * NZL + zl
    classes = table_hbm.shape[0]

    def dev(y_=None, z_=None, x_=None, core_=None):
        y_ = y if y_ is None else y_
        z_ = z if z_ is None else z_
        x_ = x if x_ is None else x_
        core_ = core if core_ is None else core_
        return {"emit": y_ * NZH + z_ // NZL, "client": (x_ * NZL + z_ % NZL) * NK + core_}

    def remote(src, dst, ssem, rsem, to):
        return pltpu.make_async_remote_copy(
            src_ref=src, dst_ref=dst, send_sem=ssem, recv_sem=rsem, device_id=to, device_id_type=MESH
        )

    barrier = pltpu.get_barrier_semaphore()

    def greet(to):
        pl.semaphore_signal(barrier, inc=1, device_id=to, device_id_type=MESH)

    def greet_client(d, carry):
        greet({"client": (c + d) % NC})
        return carry

    for d in range(1, NE):
        greet({"emit": (e + d) % NE})
    for d in range(1, NZL):
        greet(dev(z_=(1 - zh) * NZL + (zl + d) % NZL))
    lax.fori_loop(1, NC, greet_client, 0)

    ld_trunk = pltpu.make_async_copy(trunk_hbm, trunk, loc_sem.at[0])
    ld_tw = pltpu.make_async_copy(tw_hbm, tw, loc_sem.at[1])
    ld_w = pltpu.make_async_copy(emit_hbm, wfull.at[zh, y], loc_sem.at[2])
    ld_table = pltpu.make_async_copy(table_hbm, table, loc_sem.at[3])
    ld_feats = pltpu.make_async_copy(feats_hbm, feats, loc_sem.at[4])
    for cp in (ld_trunk, ld_tw, ld_w, ld_table, ld_feats):
        cp.start()

    ld_trunk.wait()
    ld_tw.wait()
    cols = dot_nt(trunk[...], tw[...]).astype(BF16)
    width = cols.shape[1]
    spread = (
        lax.broadcasted_iota(jnp.int32, (width, NK * width), 1)
        == lax.broadcasted_iota(jnp.int32, (width, NK * width), 0) + core * width
    ).astype(BF16)
    cols = dot(cols, spread).astype(BF16)
    picker = (
        lax.broadcasted_iota(jnp.int32, (CLIENTS, CLIENTS), 0) == ids_ref[...]
    ).astype(BF16)
    pre_send[...] = dot_tn(picker, cols).reshape(NC, SLOTS, NK * width)
    ld_table.wait()
    tablef[...] = jnp.zeros_like(tablef)
    tablef[0:classes, :] = table[...].astype(F32)
    for s in range(SLOTS):
        for j in range(SAMPLES // 128):
            lab[s : s + 1, j * 128 : (j + 1) * 128] = labels_ref[s * 4 + j : s * 4 + j + 1, :]
    ld_w.wait()

    pl.semaphore_wait(barrier, NE - 1 + NZL - 1 + NC - 1)

    qrow = x * QR + core * (QR // NK)
    qpart = pl.ds(pl.multiple_of(qrow, QR // NK), QR // NK)
    half = HB // NK
    cut = 64

    def hpart(first, last):
        return pl.ds(pl.multiple_of(core * half + first, cut), last - first)

    w_z = remote(wfull.at[zh, y, qpart], wfull.at[zh, y, qpart], wz_s, wz_r, dev(z_=2 * NZL - 1 - z))
    w_z.start()

    def send_pre(d, carry):
        to = (c + d) % NC
        remote(pre_send.at[to], pre_recv.at[c], pre_ssem, pre_rsem, {"client": to}).start()
        return carry

    lax.fori_loop(1, NC, send_pre, 0)
    own_pre = pltpu.make_async_copy(pre_send.at[c], pre_recv.at[c], pre_rsem)
    own_pre.start()
    w_a = []
    for d in range(1, NY):
        part = wfull.at[zh, y, hpart(0, cut)]
        cp = remote(part, part, wa_s.at[0, d - 1], wa_r.at[0, d - 1], dev(y_=(y + d) % NY))
        cp.start()
        w_a.append(cp)

    w_z.wait()
    w_b = []
    for d in range(1, NY):
        part = wfull.at[1 - zh, y, qpart]
        cp = remote(part, part, wb_s.at[d - 1], wb_r.at[d - 1], dev(y_=(y + d) % NY))
        cp.start()
        w_b.append(cp)

    def along_x(i, yy):
        copies = []
        for d in range(1, NX):
            part = wfull.at[1 - zh, yy, qpart]
            cp = remote(part, part, wc_s.at[i, d - 1], wc_r.at[i, d - 1], dev(x_=(x + d) % NX))
            cp.start()
            copies.append(cp)
        return copies

    w_c = [along_x(0, y)]

    pltpu.make_async_copy(pre_recv, pre_recv, pre_rsem).wait()
    for j in range(HID // CPAD):
        pre_own[:, j * CPAD : (j + 1) * CPAD] = pre_recv[NK * j] + pre_recv[NK * j + 1]
    pre = pre_own[...]
    sig = sigmoid(pre)
    spre[...] = pre * sig
    dp = sig * (1.0 + pre * (1.0 - sig))
    for j in range(NE):
        dpre[j] = dp[:, j * HB : (j + 1) * HB]

    live = lax.broadcasted_iota(jnp.int32, (CPAD, HB), 0) < classes

    def emit_codes(i, carry):
        s, h = i // NE, i % NE
        lanes = pl.ds(pl.multiple_of(h * HB, HB), HB)
        within = pl.ds(pl.multiple_of((h // NZH) * HB, HB), HB)
        rows = pl.ds(pl.multiple_of(s * CPAD, CPAD), CPAD)
        v = spre[pl.ds(s, 1), lanes] + tablef[:, lanes]
        g = sigmoid(v)
        a = v * g
        code[h % NZH, rows, within] = jnp.where(live, a, 0.0).astype(BF16)
        dcode[rows, lanes] = (g + a * (1.0 - g)).astype(BF16)
        return carry

    def turn(i, carry):
        s, h = i // NE, i % NE
        rows = pl.ds(pl.multiple_of(s * CPAD, CPAD), CPAD)
        within = pl.ds(pl.multiple_of((h // NZH) * HB, HB), HB)
        code_t[h, :, rows] = code[h % NZH, rows, within].T
        return carry

    lax.fori_loop(0, SLOTS * NE, emit_codes, 0, unroll=2)

    for d in range(1, NY):
        part = wfull.at[zh, y, hpart(cut, half)]
        cp = remote(part, part, wa_s.at[1, d - 1], wa_r.at[1, d - 1], dev(y_=(y + d) % NY))
        cp.start()
        w_a.append(cp)
    for d in range(1, NY):
        w_b[d - 1].wait()
        w_c.append(along_x(d, (y + NY - d) % NY))

    def to_core(i, q):
        part = wfull.at[1 - zh, :, pl.ds(pl.multiple_of(q * QR + core * (QR // NK), QR // NK), QR // NK)]
        return remote(part, part, wd_s.at[i], wd_r.at[i], dev(core_=1 - core))

    w_d = [to_core(3, x)]
    w_d[0].start()

    lax.fori_loop(0, SLOTS * NE // 2, turn, 0)
    trunk_perm[...] = dot_tn(picker, trunk[...]).astype(BF16)

    w_e = []
    for d in range(1, NY):
        w_a[d - 1].wait()
        w_a[NY - 1 + d - 1].wait()
        part = wfull.at[zh, (y + NY - d) % NY, hpart(0, half)]
        cp = remote(part, part, wd_s.at[d - 1], wd_r.at[d - 1], dev(core_=1 - core))
        cp.start()
        w_e.append(cp)
    lax.fori_loop(SLOTS * NE // 2, SLOTS * NE, turn, 0)
    for cp in w_e:
        cp.wait()

    def heads_first(m, carry):
        rows = pl.ds(pl.multiple_of(m * HB, HB), HB)
        hacc[rows, :] = dot(code[zh, rows, :], wfull[zh].reshape(HID // NZH, FEAT))
        return carry

    lax.fori_loop(0, ROWS // HB // 2, heads_first, 0)

    for d in range(1, NX):
        for copies in w_c:
            copies[d - 1].wait()
        cp = to_core(3 + d, (x + NX - d) % NX)
        cp.start()
        w_d.append(cp)
    lax.fori_loop(ROWS // HB // 2, ROWS // HB, heads_first, 0)
    for cp in w_d:
        cp.wait()

    def heads_rest(m, carry):
        rows = pl.ds(pl.multiple_of(m * HB, HB), HB)
        part = dot(code[1 - zh, rows, :], wfull[1 - zh].reshape(HID // NZH, FEAT))
        heads[rows, :] = (hacc[rows, :] + part).astype(BF16)
        return carry

    lax.fori_loop(0, ROWS // HB, heads_rest, 0)
    ld_feats.wait()

    kids = lax.broadcasted_iota(jnp.int32, (CPAD, SAMPLES), 0)
    valid = kids < classes
    kids = kids + e * classes

    def onehot_of(s):
        return jnp.logical_and(kids == lab[pl.ds(s, 1), :], valid)

    def logits_of(s, carry):
        rows = pl.ds(pl.multiple_of(s * CPAD, CPAD), CPAD)
        frows = pl.ds(pl.multiple_of(s * SAMPLES, SAMPLES), SAMPLES)
        lg = dot_nt(heads[rows, :], feats[frows, :])
        top = jnp.max(jnp.where(valid, lg, -jnp.inf), axis=0, keepdims=True)
        ex = jnp.where(valid, jnp.exp(lg - top), 0.0)
        probs[rows, :] = ex
        tops[pl.ds(s, 1), :] = top
        sums[pl.ds(s, 1), :] = jnp.sum(ex, axis=0, keepdims=True)
        tg_send[pl.ds(s, 1), :] = jnp.sum(jnp.where(onehot_of(s), lg, 0.0), axis=0, keepdims=True)
        return carry

    hs = SLOTS // 2

    def st_copies(g):
        return [
            remote(st_send.at[g], st_recv.at[g, d - 1], st_s.at[g, d - 1], st_r.at[g, d - 1], {"emit": (e + d) % NE})
            for d in range(1, NE)
        ]

    st = []
    for g in range(2):
        lax.fori_loop(g * hs, (g + 1) * hs, logits_of, 0, unroll=2)
        st_send[g] = tops[g * hs : (g + 1) * hs, :] + jnp.log(sums[g * hs : (g + 1) * hs, :])
        st.append(st_copies(g))
        for cp in st[g]:
            cp.start()

    def combine(g):
        for cp in st[g]:
            cp.wait()
        lse = st_send[g]
        gtop = lse
        for d in range(NE - 1):
            gtop = jnp.maximum(gtop, st_recv[g, d])
        total = jnp.exp(lse - gtop)
        for d in range(NE - 1):
            total += jnp.exp(st_recv[g, d] - gtop)
        top = gtop + jnp.log(total)
        part = slice(g * hs, (g + 1) * hs)
        logz[part, :] = top
        sums[part, :] = jnp.exp(tops[part, :] - top)

    def grads_of(s, carry):
        rows = pl.ds(pl.multiple_of(s * CPAD, CPAD), CPAD)
        frows = pl.ds(pl.multiple_of(s * SAMPLES, SAMPLES), SAMPLES)
        g = probs[rows, :] * sums[pl.ds(s, 1), :] - onehot_of(s).astype(F32)
        gh[rows, :] = dot((g * (1.0 / CLIENTS)).astype(BF16), feats[frows, :]).astype(BF16)
        return carry

    for g in range(2):
        combine(g)
        lax.fori_loop(g * hs, (g + 1) * hs, grads_of, 0, unroll=2)
    tg = []
    for d in range(1, NE):
        cp = remote(tg_send, tg_recv.at[d - 1], res_s.at[d - 1], res_r.at[d - 1], {"emit": (e + d) % NE})
        cp.start()
        tg.append(cp)

    def core_copy(n):
        return remote(eg.at[n, 1 - core], egr.at[n], core_s.at[n], core_r.at[n], dev(core_=1 - core))

    def x1_copy(i, d):
        to = (x + d) % NX
        part = pl.ds(pl.multiple_of(to * 32, 32), 32)
        return remote(am.at[2 * i, part], rx.at[i, d - 1], x1_s.at[i, d - 1], x1_r.at[i, d - 1], dev(x_=to))

    def along_y(i):
        return (y + 1 + 2 * i - 3 * (i // 2)) % NY

    def y1_copy(i):
        return remote(am.at[2 * i + 1], ry.at[i], y1_s.at[i], y1_r.at[i], dev(y_=along_y(i)))

    def compute_pair(i):
        yy = along_y(i)
        both = code_t[pl.ds(yy * NZH, NZH)].reshape(NZH * HB, ROWS)
        part = dot(both, gh[...]).reshape(NZH, HB // (NK * 8), NK, 8, FEAT)
        for half in (1, 0):
            n = 2 * i + half
            for k in range(NK):
                eg[n, k] = part[half, :, k].reshape(HB // NK, FEAT).astype(BF16)
            core_copy(n).start()

    def sum_codes(h):
        gc = dot_nt(gh[...], wfull[h % NZH, h // NZH])
        lanes = pl.ds(pl.multiple_of(h * HB, HB), HB)
        for s in range(SLOTS):
            part = gc[s * CPAD : (s + 1) * CPAD] * dcode[s * CPAD : (s + 1) * CPAD, lanes].astype(F32)
            gs_send[h, s : s + 1, :] = jnp.sum(part, axis=0, keepdims=True)

    def pass_on(i, last):
        for half in (1, 0):
            n = 2 * i + half
            core_copy(n).wait()
            am[n] = (eg[n, core].astype(F32) + egr[n].astype(F32)).astype(BF16)
            if half == 0:
                for d in range(1, NX):
                    x1_copy(i, d).start()
            elif not last:
                y1_copy(i).start()

    def y2_copy(i):
        return remote(bx.at[i], rxy.at[i], y2_s.at[i], y2_r.at[i], dev(y_=along_y(i)))

    xpart = pl.ds(pl.multiple_of(x * 32, 32), 32)

    def along_x_sum(i):
        for d in range(1, NX):
            x1_copy(i, d).wait()
        acc = am[2 * i, xpart, :].astype(F32)
        for d in range(NX - 1):
            acc += rx[i, d].astype(F32)
        bx[i] = acc.astype(BF16)

    compute_pair(0)
    sum_codes(0)

    def chunk_step(i, carry):
        compute_pair(i)
        pass_on(i - 1, False)
        sum_codes(i)
        return carry

    lax.fori_loop(1, NY, chunk_step, 0)
    sum_codes(NY)
    pass_on(NY - 1, True)

    def second_step(i, carry):
        sum_codes(NY + 1 + i)
        along_x_sum(i)
        y2_copy(i).start()
        return carry

    lax.fori_loop(0, NY - 1, second_step, 0)
    gs = []
    for d in range(1, NE):
        to = (e + d) % NE
        cp = remote(gs_send.at[to], gs_recv.at[d - 1], gs_s.at[d - 1], gs_r.at[d - 1], {"emit": to})
        cp.start()
        gs.append(cp)

    acc = am[2 * NY - 1].astype(F32)
    for i in range(NY - 1):
        y1_copy(i).wait()
        acc += ry[i].astype(F32)
    by[...] = acc.astype(BF16)
    x2 = []
    for d in range(1, NX):
        to = (x + d) % NX
        part = pl.ds(pl.multiple_of(to * 32, 32), 32)
        cp = remote(by.at[part], ryx.at[d - 1], x2_s.at[d - 1], x2_r.at[d - 1], dev(x_=to))
        cp.start()
        x2.append(cp)
    along_x_sum(NY - 1)

    for cp in tg:
        cp.wait()
    rest = logz[...] - tg_send[...]
    for d in range(NE - 1):
        rest = rest - tg_recv[d]
    for s in range(SLOTS):
        for j in range(SAMPLES // 128):
            loss_ref[s * 4 + j : s * 4 + j + 1, :] = rest[s : s + 1, j * 128 : (j + 1) * 128]

    for cp in gs:
        cp.wait()
    block = gs_send[e]
    for d in range(NE - 1):
        block = block + gs_recv[d]
    gp_send[...] = (block * dpre[e]).astype(BF16)

    def send_gp(d, carry):
        remote(gp_send, gp_recv.at[c], gp_ssem, gp_rsem, {"client": (c + d) % NC}).start()
        return carry

    lax.fori_loop(1, NC, send_gp, 0)
    own_gp = pltpu.make_async_copy(gp_send, gp_recv.at[c], gp_rsem)
    own_gp.start()

    for i in range(NY - 1):
        y2_copy(i).wait()
    acc = bx[NY - 1].astype(F32)
    for d in range(NY - 1):
        acc += rxy[d].astype(F32)
    cz[0:NZL] = acc.astype(BF16).reshape(NZL, 8, FEAT)
    for cp in x2:
        cp.wait()
    acc = by[xpart, :].astype(F32)
    for d in range(NX - 1):
        acc += ryx[d].astype(F32)
    cz[NZL:] = acc.astype(BF16).reshape(NZL, 8, FEAT)
    nz = NZH * NZL
    zs = []
    for d in range(1, nz):
        to = (z + d) % nz
        cp = remote(cz.at[to], rz.at[d - 1], z_s.at[d - 1], z_r.at[d - 1], dev(z_=to))
        cp.start()
        zs.append(cp)

    pltpu.make_async_copy(gp_recv, gp_recv, gp_rsem).wait()
    select = (
        lax.broadcasted_iota(jnp.int32, (8, HB), 1) == lax.broadcasted_iota(jnp.int32, (8, HB), 0) + c * 8
    ).astype(BF16)
    mine = dot_nt(select, gp_recv[...].reshape(CLIENTS, HB)).astype(BF16)
    tgrad_ref[...] = dot(mine, trunk_perm[...])

    for cp in zs:
        cp.wait()
    acc = cz[z].astype(F32)
    for d in range(nz - 1):
        acc += rz[d].astype(F32)
    egrad_ref[...] = acc

    remote(pre_send.at[0 : NC - 1], pre_recv.at[0 : NC - 1], pre_ssem, pre_rsem, {"client": (c + 1) % NC}).wait_send()
    remote(gp_recv.at[0 : NC - 1], gp_recv.at[0 : NC - 1], gp_ssem, gp_rsem, {"client": (c + 1) % NC}).wait_send()


def hand_over(loss_in, egrad_in, tgrad_in, loss_ref, egrad_ref, tgrad_ref):
    loss_ref[...] = loss_in[...]
    egrad_ref[...] = egrad_in[...]
    tgrad_ref[...] = tgrad_in[...]


def per_device(features, labels, client_ids, trunk_in, trunk_weight, class_table, emit_weight):
    vm = pltpu.VMEM
    dma = pltpu.SemaphoreType.DMA
    half = HB // NK
    scratch = [
        vm((SLOTS * SAMPLES, FEAT), BF16), vm((SLOTS, SAMPLES), jnp.int32), vm((CLIENTS, HID), BF16), vm((trunk_weight.shape[1], HID), BF16),
        vm(class_table.shape, BF16), vm((CPAD, HID), F32), vm((NZH, NY, HB, FEAT), BF16),
        vm((NC, SLOTS, CPAD), F32), vm((NC, SLOTS, CPAD), F32), vm((SLOTS, HID), F32), vm((SLOTS, HID), F32),
        vm((NE, SLOTS, HB), F32),
        vm((NZH, ROWS, HID // NZH), BF16), vm((NE, HB, ROWS), BF16), vm((ROWS, HID), BF16), vm((ROWS, FEAT), F32),
        vm((ROWS, FEAT), BF16),
        vm((ROWS, SAMPLES), F32), vm((SLOTS, SAMPLES), F32),
        vm((SLOTS, SAMPLES), F32), vm((SLOTS, SAMPLES), F32),
        vm((2, SLOTS // 2, SAMPLES), F32), vm((2, NE - 1, SLOTS // 2, SAMPLES), F32), vm((SLOTS, SAMPLES), F32),
        vm((NE - 1, SLOTS, SAMPLES), F32),
        vm((ROWS, FEAT), BF16), vm((NE, NK, half, FEAT), BF16), vm((NE, half, FEAT), BF16), vm((NE, half, FEAT), BF16),
        vm((NY, NX - 1, 32, FEAT), BF16), vm((NY - 1, half, FEAT), BF16),
        vm((NY, 32, FEAT), BF16), vm((NY - 1, 32, FEAT), BF16), vm((half, FEAT), BF16), vm((NX - 1, 32, FEAT), BF16),
        vm((NZH * NZL, 8, FEAT), BF16), vm((NZH * NZL - 1, 8, FEAT), BF16),
        vm((NE, SLOTS, HB), F32), vm((NE - 1, SLOTS, HB), F32), vm((SLOTS, HB), BF16), vm((NC, SLOTS, HB), BF16),
        vm((CLIENTS, HID), BF16),
        dma((5,)), dma, dma,
        dma((2, 3)), dma((2, 3)), dma, dma, dma((3,)), dma((3,)), dma((4, 3)), dma((4, 3)), dma((7,)), dma((7,)),
        dma((2, 7)), dma((2, 7)), dma((7,)), dma((7,)), dma((8,)), dma((8,)),
        dma((4, 3)), dma((4, 3)), dma((3,)), dma((3,)), dma((3,)), dma((3,)), dma((3,)), dma((3,)), dma((7,)), dma((7,)),
        dma((7,)), dma((7,)), dma, dma,
    ]
    hbm = pl.BlockSpec(memory_space=pl.ANY)
    here = pl.BlockSpec(memory_space=pltpu.VMEM)
    loss, egrad, tgrad = pl.pallas_call(
        step_kernel,
        name="hyper_step",
        out_shape=(
            jax.ShapeDtypeStruct((SLOTS * SAMPLES // 128, 128), F32),
            jax.ShapeDtypeStruct((HID // (NE * NC), FEAT), F32),
            jax.ShapeDtypeStruct((HID // (NE * NC), HID), F32),
        ),
        in_specs=[hbm, here, here, hbm, hbm, hbm, hbm],
        out_specs=(here, here, here),
        scratch_shapes=scratch,
        compiler_params=pltpu.CompilerParams(collective_id=0, has_side_effects=True, vmem_limit_bytes=56 << 20),
    )(
        features, labels.reshape(SLOTS * SAMPLES // 128, 128), client_ids.reshape(1, CLIENTS), trunk_in, trunk_weight.T,
        class_table, emit_weight,
    )
    outs = (loss, egrad, tgrad)
    loss, egrad, tgrad = pl.pallas_call(
        hand_over,
        name="hand_over",
        out_shape=tuple(jax.ShapeDtypeStruct(o.shape, o.dtype) for o in outs),
        in_specs=[here] * 3,
        out_specs=(here,) * 3,
    )(*outs)
    return loss.reshape(SLOTS * SAMPLES), egrad, tgrad.T


def solution(mesh):
    return jax.shard_map(
        per_device,
        mesh=mesh,
        in_specs=(
            P("client", None),
            P("client"),
            P(),
            P(),
            P(None, "client"),
            P("emit", None),
            P("emit", None),
        ),
        out_specs=(P("client"), P(("emit", "client"), None), P(None, ("emit", "client"))),
        check_vma=False,
    )
```

```python
import jax
import jax.numpy as jnp
from jax import lax
from jax.experimental import pallas as pl
from jax.experimental.pallas import tpu as pltpu
from jax.sharding import PartitionSpec as P

MESH = pl.DeviceIdType.MESH
BF16 = jnp.bfloat16
F32 = jnp.float32

NY, NZH, NX, NZL, NK = 4, 2, 4, 4, 2
NE, NC = NY * NZH, NX * NZL * NK
SLOTS = 8
SAMPLES = 512
CPAD = 128
ROWS = SLOTS * CPAD
HID = 2048
FEAT = 768
CLIENTS = 256
HB = HID // NE
QR = HB // NX


def dot(a, b):
    return jnp.dot(a, b, preferred_element_type=F32)


def dot_nt(a, b):
    return lax.dot_general(a, b, (((1,), (1,)), ((), ())), preferred_element_type=F32)


def dot_tn(a, b):
    return lax.dot_general(a, b, (((0,), (0,)), ((), ())), preferred_element_type=F32)


def sigmoid(v):
    return 0.5 * jnp.tanh(0.5 * v) + 0.5


def step_kernel(
    feats_hbm, labels_ref, ids_ref, trunk_hbm, tw_hbm, table_hbm, emit_hbm,
    loss_ref, egrad_ref, tgrad_ref,
    feats, lab, trunk, tw, table, tablef, wfull,
    pre_send, pre_recv, pre_own, spre, dpre,
    code, code_t, dcode, hacc, heads, probs, tops,
    sums, logz, st_send, st_recv, tg_send, tg_recv,
    gh, eg, egr, am, rx, ry, bx, rxy, by, ryx, cz, rz,
    gs_send, gs_recv, gp_send, gp_recv, trunk_perm,
    loc_sem, pre_ssem, pre_rsem,
    wa_s, wa_r, wz_s, wz_r, wb_s, wb_r, wc_s, wc_r, wd_s, wd_r,
    st_s, st_r, res_s, res_r, core_s, core_r,
    x1_s, x1_r, y1_s, y1_r, x2_s, x2_r, y2_s, y2_r, z_s, z_r,
    gs_s, gs_r, gp_ssem, gp_rsem,
):
    e = lax.axis_index("emit")
    c = lax.axis_index("client")
    y, zh = e // NZH, e % NZH
    x, zl, core = c // (NZL * NK), (c // NK) % NZL, c % NK
    z = zh * NZL + zl
    classes = table_hbm.shape[0]

    def dev(y_=None, z_=None, x_=None, core_=None):
        y_ = y if y_ is None else y_
        z_ = z if z_ is None else z_
        x_ = x if x_ is None else x_
        core_ = core if core_ is None else core_
        return {"emit": y_ * NZH + z_ // NZL, "client": (x_ * NZL + z_ % NZL) * NK + core_}

    def remote(src, dst, ssem, rsem, to):
        return pltpu.make_async_remote_copy(
            src_ref=src, dst_ref=dst, send_sem=ssem, recv_sem=rsem, device_id=to, device_id_type=MESH
        )

    barrier = pltpu.get_barrier_semaphore()

    def greet(to):
        pl.semaphore_signal(barrier, inc=1, device_id=to, device_id_type=MESH)

    def greet_client(d, carry):
        greet({"client": (c + d) % NC})
        return carry

    for d in range(1, NE):
        greet({"emit": (e + d) % NE})
    for d in range(1, NZL):
        greet(dev(z_=(1 - zh) * NZL + (zl + d) % NZL))
    lax.fori_loop(1, NC, greet_client, 0)

    ld_trunk = pltpu.make_async_copy(trunk_hbm, trunk, loc_sem.at[0])
    ld_tw = pltpu.make_async_copy(tw_hbm, tw, loc_sem.at[1])
    ld_w = pltpu.make_async_copy(emit_hbm, wfull.at[zh, y], loc_sem.at[2])
    ld_table = pltpu.make_async_copy(table_hbm, table, loc_sem.at[3])
    ld_feats = pltpu.make_async_copy(feats_hbm, feats, loc_sem.at[4])
    for cp in (ld_trunk, ld_tw, ld_w, ld_table, ld_feats):
        cp.start()

    ld_trunk.wait()
    ld_tw.wait()
    cols = dot_nt(trunk[...], tw[...]).astype(BF16)
    width = cols.shape[1]
    spread = (
        lax.broadcasted_iota(jnp.int32, (width, NK * width), 1)
        == lax.broadcasted_iota(jnp.int32, (width, NK * width), 0) + core * width
    ).astype(BF16)
    cols = dot(cols, spread).astype(BF16)
    picker = (
        lax.broadcasted_iota(jnp.int32, (CLIENTS, CLIENTS), 0) == ids_ref[...]
    ).astype(BF16)
    pre_send[...] = dot_tn(picker, cols).reshape(NC, SLOTS, NK * width)
    ld_table.wait()
    tablef[...] = jnp.zeros_like(tablef)
    tablef[0:classes, :] = table[...].astype(F32)
    for s in range(SLOTS):
        for j in range(SAMPLES // 128):
            lab[s : s + 1, j * 128 : (j + 1) * 128] = labels_ref[s * 4 + j : s * 4 + j + 1, :]
    ld_w.wait()

    pl.semaphore_wait(barrier, NE - 1 + NZL - 1 + NC - 1)

    qrow = x * QR + core * (QR // NK)
    qpart = pl.ds(pl.multiple_of(qrow, QR // NK), QR // NK)
    half = HB // NK
    cut = 64

    def hpart(first, last):
        return pl.ds(pl.multiple_of(core * half + first, cut), last - first)

    w_z = remote(wfull.at[zh, y, qpart], wfull.at[zh, y, qpart], wz_s, wz_r, dev(z_=2 * NZL - 1 - z))
    w_z.start()

    def send_pre(d, carry):
        to = (c + d) % NC
        remote(pre_send.at[to], pre_recv.at[c], pre_ssem, pre_rsem, {"client": to}).start()
        return carry

    lax.fori_loop(1, NC, send_pre, 0)
    own_pre = pltpu.make_async_copy(pre_send.at[c], pre_recv.at[c], pre_rsem)
    own_pre.start()
    w_a = []
    for d in range(1, NY):
        part = wfull.at[zh, y, hpart(0, cut)]
        cp = remote(part, part, wa_s.at[0, d - 1], wa_r.at[0, d - 1], dev(y_=(y + d) % NY))
        cp.start()
        w_a.append(cp)

    w_z.wait()
    w_b = []
    for d in range(1, NY):
        part = wfull.at[1 - zh, y, qpart]
        cp = remote(part, part, wb_s.at[d - 1], wb_r.at[d - 1], dev(y_=(y + d) % NY))
        cp.start()
        w_b.append(cp)

    def along_x(i, yy):
        copies = []
        for d in range(1, NX):
            part = wfull.at[1 - zh, yy, qpart]
            cp = remote(part, part, wc_s.at[i, d - 1], wc_r.at[i, d - 1], dev(x_=(x + d) % NX))
            cp.start()
            copies.append(cp)
        return copies

    w_c = [along_x(0, y)]

    pltpu.make_async_copy(pre_recv, pre_recv, pre_rsem).wait()
    for j in range(HID // CPAD):
        pre_own[:, j * CPAD : (j + 1) * CPAD] = pre_recv[NK * j] + pre_recv[NK * j + 1]
    pre = pre_own[...]
    sig = sigmoid(pre)
    spre[...] = pre * sig
    dp = sig * (1.0 + pre * (1.0 - sig))
    for j in range(NE):
        dpre[j] = dp[:, j * HB : (j + 1) * HB]

    live = lax.broadcasted_iota(jnp.int32, (CPAD, HB), 0) < classes

    def emit_codes(i, carry):
        s, h = i // NE, i % NE
        lanes = pl.ds(pl.multiple_of(h * HB, HB), HB)
        within = pl.ds(pl.multiple_of((h // NZH) * HB, HB), HB)
        rows = pl.ds(pl.multiple_of(s * CPAD, CPAD), CPAD)
        v = spre[pl.ds(s, 1), lanes] + tablef[:, lanes]
        g = sigmoid(v)
        a = v * g
        code[h % NZH, rows, within] = jnp.where(live, a, 0.0).astype(BF16)
        dcode[rows, lanes] = (g + a * (1.0 - g)).astype(BF16)
        return carry

    def turn(i, carry):
        s, h = i // NE, i % NE
        rows = pl.ds(pl.multiple_of(s * CPAD, CPAD), CPAD)
        within = pl.ds(pl.multiple_of((h // NZH) * HB, HB), HB)
        code_t[h, :, rows] = code[h % NZH, rows, within].T
        return carry

    lax.fori_loop(0, SLOTS * NE, emit_codes, 0, unroll=2)

    for d in range(1, NY):
        part = wfull.at[zh, y, hpart(cut, half)]
        cp = remote(part, part, wa_s.at[1, d - 1], wa_r.at[1, d - 1], dev(y_=(y + d) % NY))
        cp.start()
        w_a.append(cp)
    for d in range(1, NY):
        w_b[d - 1].wait()
        w_c.append(along_x(d, (y + NY - d) % NY))

    def to_core(i, q):
        part = wfull.at[1 - zh, :, pl.ds(pl.multiple_of(q * QR + core * (QR // NK), QR // NK), QR // NK)]
        return remote(part, part, wd_s.at[i], wd_r.at[i], dev(core_=1 - core))

    w_d = [to_core(3, x)]
    w_d[0].start()

    lax.fori_loop(0, SLOTS * NE // 2, turn, 0)
    trunk_perm[...] = dot_tn(picker, trunk[...]).astype(BF16)

    w_e = []
    for d in range(1, NY):
        w_a[d - 1].wait()
        w_a[NY - 1 + d - 1].wait()
        part = wfull.at[zh, (y + NY - d) % NY, hpart(0, half)]
        cp = remote(part, part, wd_s.at[d - 1], wd_r.at[d - 1], dev(core_=1 - core))
        cp.start()
        w_e.append(cp)
    lax.fori_loop(SLOTS * NE // 2, SLOTS * NE, turn, 0)
    for cp in w_e:
        cp.wait()

    def heads_first(m, carry):
        rows = pl.ds(pl.multiple_of(m * HB, HB), HB)
        hacc[rows, :] = dot(code[zh, rows, :], wfull[zh].reshape(HID // NZH, FEAT))
        return carry

    lax.fori_loop(0, ROWS // HB // 2, heads_first, 0)

    for d in range(1, NX):
        for copies in w_c:
            copies[d - 1].wait()
        cp = to_core(3 + d, (x + NX - d) % NX)
        cp.start()
        w_d.append(cp)
    lax.fori_loop(ROWS // HB // 2, ROWS // HB, heads_first, 0)
    for cp in w_d:
        cp.wait()

    def heads_rest(m, carry):
        rows = pl.ds(pl.multiple_of(m * HB, HB), HB)
        part = dot(code[1 - zh, rows, :], wfull[1 - zh].reshape(HID // NZH, FEAT))
        heads[rows, :] = (hacc[rows, :] + part).astype(BF16)
        return carry

    lax.fori_loop(0, ROWS // HB, heads_rest, 0)
    ld_feats.wait()

    kids = lax.broadcasted_iota(jnp.int32, (CPAD, SAMPLES), 0)
    valid = kids < classes
    kids = kids + e * classes

    def onehot_of(s):
        return jnp.logical_and(kids == lab[pl.ds(s, 1), :], valid)

    def logits_of(s, carry):
        rows = pl.ds(pl.multiple_of(s * CPAD, CPAD), CPAD)
        frows = pl.ds(pl.multiple_of(s * SAMPLES, SAMPLES), SAMPLES)
        lg = dot_nt(heads[rows, :], feats[frows, :])
        top = jnp.max(jnp.where(valid, lg, -jnp.inf), axis=0, keepdims=True)
        ex = jnp.where(valid, jnp.exp(lg - top), 0.0)
        probs[rows, :] = ex
        tops[pl.ds(s, 1), :] = top
        sums[pl.ds(s, 1), :] = jnp.sum(ex, axis=0, keepdims=True)
        tg_send[pl.ds(s, 1), :] = jnp.sum(jnp.where(onehot_of(s), lg, 0.0), axis=0, keepdims=True)
        return carry

    hs = SLOTS // 2

    def st_copies(g):
        return [
            remote(st_send.at[g], st_recv.at[g, d - 1], st_s.at[g, d - 1], st_r.at[g, d - 1], {"emit": (e + d) % NE})
            for d in range(1, NE)
        ]

    st = []
    for g in range(2):
        lax.fori_loop(g * hs, (g + 1) * hs, logits_of, 0, unroll=2)
        st_send[g] = tops[g * hs : (g + 1) * hs, :] + jnp.log(sums[g * hs : (g + 1) * hs, :])
        st.append(st_copies(g))
        for cp in st[g]:
            cp.start()

    def combine(g):
        for cp in st[g]:
            cp.wait()
        lse = st_send[g]
        gtop = lse
        for d in range(NE - 1):
            gtop = jnp.maximum(gtop, st_recv[g, d])
        total = jnp.exp(lse - gtop)
        for d in range(NE - 1):
            total += jnp.exp(st_recv[g, d] - gtop)
        top = gtop + jnp.log(total)
        part = slice(g * hs, (g + 1) * hs)
        logz[part, :] = top
        sums[part, :] = jnp.exp(tops[part, :] - top)

    def grads_of(s, carry):
        rows = pl.ds(pl.multiple_of(s * CPAD, CPAD), CPAD)
        frows = pl.ds(pl.multiple_of(s * SAMPLES, SAMPLES), SAMPLES)
        g = probs[rows, :] * sums[pl.ds(s, 1), :] - onehot_of(s).astype(F32)
        gh[rows, :] = dot((g * (1.0 / CLIENTS)).astype(BF16), feats[frows, :]).astype(BF16)
        return carry

    for g in range(2):
        combine(g)
        lax.fori_loop(g * hs, (g + 1) * hs, grads_of, 0, unroll=2)
    tg = []
    for d in range(1, NE):
        cp = remote(tg_send, tg_recv.at[d - 1], res_s.at[d - 1], res_r.at[d - 1], {"emit": (e + d) % NE})
        cp.start()
        tg.append(cp)

    def core_copy(n):
        return remote(eg.at[n, 1 - core], egr.at[n], core_s.at[n], core_r.at[n], dev(core_=1 - core))

    def x1_copy(i, d):
        to = (x + d) % NX
        part = pl.ds(pl.multiple_of(to * 32, 32), 32)
        return remote(am.at[2 * i, part], rx.at[i, d - 1], x1_s.at[i, d - 1], x1_r.at[i, d - 1], dev(x_=to))

    def along_y(i):
        return (y + 1 + 2 * i - 3 * (i // 2)) % NY

    def y1_copy(i):
        return remote(am.at[2 * i + 1], ry.at[i], y1_s.at[i], y1_r.at[i], dev(y_=along_y(i)))

    def compute_chunk(i, half):
        n = 2 * i + half
        part = dot(code_t[along_y(i) * NZH + half], gh[...]).reshape(HB // (NK * 8), NK, 8, FEAT)
        for k in range(NK):
            eg[n, k] = part[:, k].reshape(HB // NK, FEAT).astype(BF16)
        core_copy(n).start()

    def sum_codes(h):
        gc = dot_nt(gh[...], wfull[h % NZH, h // NZH])
        lanes = pl.ds(pl.multiple_of(h * HB, HB), HB)
        for s in range(SLOTS):
            part = gc[s * CPAD : (s + 1) * CPAD] * dcode[s * CPAD : (s + 1) * CPAD, lanes].astype(F32)
            gs_send[h, s : s + 1, :] = jnp.sum(part, axis=0, keepdims=True)

    def pass_on(i, half):
        n = 2 * i + half
        core_copy(n).wait()
        am[n] = (eg[n, core].astype(F32) + egr[n].astype(F32)).astype(BF16)
        if half == 0:
            for d in range(1, NX):
                x1_copy(i, d).start()

    def pass_on_y(i):
        pass_on(i, 1)
        y1_copy(i).start()

    def y2_copy(i):
        return remote(bx.at[i], rxy.at[i], y2_s.at[i], y2_r.at[i], dev(y_=along_y(i)))

    xpart = pl.ds(pl.multiple_of(x * 32, 32), 32)

    def along_x_sum(i):
        for d in range(1, NX):
            x1_copy(i, d).wait()
        acc = am[2 * i, xpart, :].astype(F32)
        for d in range(NX - 1):
            acc += rx[i, d].astype(F32)
        bx[i] = acc.astype(BF16)

    compute_chunk(0, 1)
    compute_chunk(0, 0)
    compute_chunk(1, 1)

    def chunk_step(j, carry):
        compute_chunk(j + 1, 0)
        pass_on_y(j)
        compute_chunk(j + 2, 1)
        pass_on(j, 0)
        return carry

    lax.fori_loop(0, NY - 2, chunk_step, 0)
    compute_chunk(NY - 1, 0)
    pass_on_y(NY - 2)
    sum_codes(0)
    pass_on(NY - 2, 0)
    sum_codes(1)
    pass_on(NY - 1, 0)
    pass_on(NY - 1, 1)

    def sum_step(h, carry):
        sum_codes(h)
        return carry

    lax.fori_loop(2, NE, sum_step, 0)

    gs = []
    for d in range(1, NE):
        to = (e + d) % NE
        cp = remote(gs_send.at[to], gs_recv.at[d - 1], gs_s.at[d - 1], gs_r.at[d - 1], {"emit": to})
        cp.start()
        gs.append(cp)

    def second_step(i, carry):
        along_x_sum(i)
        y2_copy(i).start()
        return carry

    lax.fori_loop(0, NY - 1, second_step, 0)
    acc = am[2 * NY - 1].astype(F32)
    for i in range(NY - 1):
        y1_copy(i).wait()
        acc += ry[i].astype(F32)
    by[...] = acc.astype(BF16)
    x2 = []
    for d in range(1, NX):
        to = (x + d) % NX
        part = pl.ds(pl.multiple_of(to * 32, 32), 32)
        cp = remote(by.at[part], ryx.at[d - 1], x2_s.at[d - 1], x2_r.at[d - 1], dev(x_=to))
        cp.start()
        x2.append(cp)
    along_x_sum(NY - 1)

    for cp in gs:
        cp.wait()
    block = gs_send[e]
    for d in range(NE - 1):
        block = block + gs_recv[d]
    gp_send[...] = (block * dpre[e]).astype(BF16)

    def send_gp(d, carry):
        remote(gp_send, gp_recv.at[c], gp_ssem, gp_rsem, {"client": (c + d) % NC}).start()
        return carry

    lax.fori_loop(1, NC, send_gp, 0)
    own_gp = pltpu.make_async_copy(gp_send, gp_recv.at[c], gp_rsem)
    own_gp.start()

    for i in range(NY - 1):
        y2_copy(i).wait()
    acc = bx[NY - 1].astype(F32)
    for d in range(NY - 1):
        acc += rxy[d].astype(F32)
    cz[0:NZL] = acc.astype(BF16).reshape(NZL, 8, FEAT)
    for cp in x2:
        cp.wait()
    acc = by[xpart, :].astype(F32)
    for d in range(NX - 1):
        acc += ryx[d].astype(F32)
    cz[NZL:] = acc.astype(BF16).reshape(NZL, 8, FEAT)
    nz = NZH * NZL
    zs = []
    for d in range(1, nz):
        to = (z + d) % nz
        cp = remote(cz.at[to], rz.at[d - 1], z_s.at[d - 1], z_r.at[d - 1], dev(z_=to))
        cp.start()
        zs.append(cp)

    for cp in tg:
        cp.wait()
    rest = logz[...] - tg_send[...]
    for d in range(NE - 1):
        rest = rest - tg_recv[d]
    for s in range(SLOTS):
        for j in range(SAMPLES // 128):
            loss_ref[s * 4 + j : s * 4 + j + 1, :] = rest[s : s + 1, j * 128 : (j + 1) * 128]

    pltpu.make_async_copy(gp_recv, gp_recv, gp_rsem).wait()
    select = (
        lax.broadcasted_iota(jnp.int32, (8, HB), 1) == lax.broadcasted_iota(jnp.int32, (8, HB), 0) + c * 8
    ).astype(BF16)
    mine = dot_nt(select, gp_recv[...].reshape(CLIENTS, HB)).astype(BF16)
    tgrad_ref[...] = dot(mine, trunk_perm[...])

    for cp in zs:
        cp.wait()
    acc = cz[z].astype(F32)
    for d in range(nz - 1):
        acc += rz[d].astype(F32)
    egrad_ref[...] = acc

    remote(pre_send.at[0 : NC - 1], pre_recv.at[0 : NC - 1], pre_ssem, pre_rsem, {"client": (c + 1) % NC}).wait_send()
    remote(gp_recv.at[0 : NC - 1], gp_recv.at[0 : NC - 1], gp_ssem, gp_rsem, {"client": (c + 1) % NC}).wait_send()


def hand_over(loss_in, egrad_in, tgrad_in, loss_ref, egrad_ref, tgrad_ref):
    loss_ref[...] = loss_in[...]
    egrad_ref[...] = egrad_in[...]
    tgrad_ref[...] = tgrad_in[...]


def per_device(features, labels, client_ids, trunk_in, trunk_weight, class_table, emit_weight):
    vm = pltpu.VMEM
    dma = pltpu.SemaphoreType.DMA
    half = HB // NK
    scratch = [
        vm((SLOTS * SAMPLES, FEAT), BF16), vm((SLOTS, SAMPLES), jnp.int32), vm((CLIENTS, HID), BF16), vm((trunk_weight.shape[1], HID), BF16),
        vm(class_table.shape, BF16), vm((CPAD, HID), F32), vm((NZH, NY, HB, FEAT), BF16),
        vm((NC, SLOTS, CPAD), F32), vm((NC, SLOTS, CPAD), F32), vm((SLOTS, HID), F32), vm((SLOTS, HID), F32),
        vm((NE, SLOTS, HB), F32),
        vm((NZH, ROWS, HID // NZH), BF16), vm((NE, HB, ROWS), BF16), vm((ROWS, HID), BF16), vm((ROWS, FEAT), F32),
        vm((ROWS, FEAT), BF16),
        vm((ROWS, SAMPLES), F32), vm((SLOTS, SAMPLES), F32),
        vm((SLOTS, SAMPLES), F32), vm((SLOTS, SAMPLES), F32),
        vm((2, SLOTS // 2, SAMPLES), F32), vm((2, NE - 1, SLOTS // 2, SAMPLES), F32), vm((SLOTS, SAMPLES), F32),
        vm((NE - 1, SLOTS, SAMPLES), F32),
        vm((ROWS, FEAT), BF16), vm((NE, NK, half, FEAT), BF16), vm((NE, half, FEAT), BF16), vm((NE, half, FEAT), BF16),
        vm((NY, NX - 1, 32, FEAT), BF16), vm((NY - 1, half, FEAT), BF16),
        vm((NY, 32, FEAT), BF16), vm((NY - 1, 32, FEAT), BF16), vm((half, FEAT), BF16), vm((NX - 1, 32, FEAT), BF16),
        vm((NZH * NZL, 8, FEAT), BF16), vm((NZH * NZL - 1, 8, FEAT), BF16),
        vm((NE, SLOTS, HB), F32), vm((NE - 1, SLOTS, HB), F32), vm((SLOTS, HB), BF16), vm((NC, SLOTS, HB), BF16),
        vm((CLIENTS, HID), BF16),
        dma((5,)), dma, dma,
        dma((2, 3)), dma((2, 3)), dma, dma, dma((3,)), dma((3,)), dma((4, 3)), dma((4, 3)), dma((7,)), dma((7,)),
        dma((2, 7)), dma((2, 7)), dma((7,)), dma((7,)), dma((8,)), dma((8,)),
        dma((4, 3)), dma((4, 3)), dma((3,)), dma((3,)), dma((3,)), dma((3,)), dma((3,)), dma((3,)), dma((7,)), dma((7,)),
        dma((7,)), dma((7,)), dma, dma,
    ]
    hbm = pl.BlockSpec(memory_space=pl.ANY)
    here = pl.BlockSpec(memory_space=pltpu.VMEM)
    loss, egrad, tgrad = pl.pallas_call(
        step_kernel,
        name="hyper_step",
        out_shape=(
            jax.ShapeDtypeStruct((SLOTS * SAMPLES // 128, 128), F32),
            jax.ShapeDtypeStruct((HID // (NE * NC), FEAT), F32),
            jax.ShapeDtypeStruct((HID // (NE * NC), HID), F32),
        ),
        in_specs=[hbm, here, here, hbm, hbm, hbm, hbm],
        out_specs=(here, here, here),
        scratch_shapes=scratch,
        compiler_params=pltpu.CompilerParams(collective_id=0, has_side_effects=True, vmem_limit_bytes=56 << 20),
    )(
        features, labels.reshape(SLOTS * SAMPLES // 128, 128), client_ids.reshape(1, CLIENTS), trunk_in, trunk_weight.T,
        class_table, emit_weight,
    )
    outs = (loss, egrad, tgrad)
    loss, egrad, tgrad = pl.pallas_call(
        hand_over,
        name="hand_over",
        out_shape=tuple(jax.ShapeDtypeStruct(o.shape, o.dtype) for o in outs),
        in_specs=[here] * 3,
        out_specs=(here,) * 3,
    )(*outs)
    return loss.reshape(SLOTS * SAMPLES), egrad, tgrad.T


def solution(mesh):
    return jax.shard_map(
        per_device,
        mesh=mesh,
        in_specs=(
            P("client", None),
            P("client"),
            P(),
            P(),
            P(None, "client"),
            P("emit", None),
            P("emit", None),
        ),
        out_specs=(P("client"), P(("emit", "client"), None), P(None, ("emit", "client"))),
        check_vma=False,
    )
```

```python
import jax
import jax.numpy as jnp
from jax import lax
from jax.experimental import pallas as pl
from jax.experimental.pallas import tpu as pltpu
from jax.sharding import PartitionSpec as P

MESH = pl.DeviceIdType.MESH
BF16 = jnp.bfloat16
F32 = jnp.float32

NY, NZH, NX, NZL, NK = 4, 2, 4, 4, 2
NE, NC = NY * NZH, NX * NZL * NK
SLOTS = 8
SAMPLES = 512
GROUPS = 4
CPAD = 128
ROWS = SLOTS * CPAD
HID = 2048
FEAT = 768
CLIENTS = 256
HB = HID // NE
QR = HB // NX


def dot(a, b):
    return jnp.dot(a, b, preferred_element_type=F32)


def dot_nt(a, b):
    return lax.dot_general(a, b, (((1,), (1,)), ((), ())), preferred_element_type=F32)


def dot_tn(a, b):
    return lax.dot_general(a, b, (((0,), (0,)), ((), ())), preferred_element_type=F32)


def sigmoid(v):
    return 0.5 * jnp.tanh(0.5 * v) + 0.5


def step_kernel(
    feats_hbm, labels_ref, ids_ref, trunk_hbm, tw_hbm, table_hbm, emit_hbm,
    loss_ref, egrad_ref, tgrad_ref,
    feats, lab, trunk, tw, table, tablef, wfull,
    pre_send, pre_recv, pre_own, spre, dpre,
    code, code_t, dcode, hacc, heads, probs, tops,
    sums, logz, st_send, st_recv, tg_send, tg_recv,
    gh, eg, egr, am, rx, ry, bx, rxy, by, ryx, cz, rz,
    gs_send, gs_half, gs_recv, gp_send, gp_recv, trunk_perm,
    loc_sem, pre_ssem, pre_rsem,
    wa_s, wa_r, wz_s, wz_r, wb_s, wb_r, wc_s, wc_r, wd_s, wd_r,
    st_s, st_r, res_s, res_r, core_s, core_r,
    x1_s, x1_r, y1_s, y1_r, x2_s, x2_r, y2_s, y2_r, z_s, z_r,
    gs_s, gs_r, gp_ssem, gp_rsem,
):
    e = lax.axis_index("emit")
    c = lax.axis_index("client")
    y, zh = e // NZH, e % NZH
    x, zl, core = c // (NZL * NK), (c // NK) % NZL, c % NK
    z = zh * NZL + zl
    classes = table_hbm.shape[0]

    def dev(y_=None, z_=None, x_=None, core_=None):
        y_ = y if y_ is None else y_
        z_ = z if z_ is None else z_
        x_ = x if x_ is None else x_
        core_ = core if core_ is None else core_
        return {"emit": y_ * NZH + z_ // NZL, "client": (x_ * NZL + z_ % NZL) * NK + core_}

    def remote(src, dst, ssem, rsem, to):
        return pltpu.make_async_remote_copy(
            src_ref=src, dst_ref=dst, send_sem=ssem, recv_sem=rsem, device_id=to, device_id_type=MESH
        )

    barrier = pltpu.get_barrier_semaphore()

    def greet(to):
        pl.semaphore_signal(barrier, inc=1, device_id=to, device_id_type=MESH)

    def greet_client(d, carry):
        greet({"client": (c + d) % NC})
        return carry

    for d in range(1, NE):
        greet({"emit": (e + d) % NE})
    for d in range(1, NZL):
        greet(dev(z_=(1 - zh) * NZL + (zl + d) % NZL))
    lax.fori_loop(1, NC, greet_client, 0)

    ld_trunk = pltpu.make_async_copy(trunk_hbm, trunk, loc_sem.at[0])
    ld_tw = pltpu.make_async_copy(tw_hbm, tw, loc_sem.at[1])
    ld_w = pltpu.make_async_copy(emit_hbm, wfull.at[zh, y], loc_sem.at[2])
    ld_table = pltpu.make_async_copy(table_hbm, table, loc_sem.at[3])
    ld_feats = pltpu.make_async_copy(feats_hbm, feats, loc_sem.at[4])
    for cp in (ld_trunk, ld_tw, ld_w, ld_table, ld_feats):
        cp.start()

    ld_trunk.wait()
    ld_tw.wait()
    cols = dot_nt(trunk[...], tw[...]).astype(BF16)
    width = cols.shape[1]
    spread = (
        lax.broadcasted_iota(jnp.int32, (width, NK * width), 1)
        == lax.broadcasted_iota(jnp.int32, (width, NK * width), 0) + core * width
    ).astype(BF16)
    cols = dot(cols, spread).astype(BF16)
    picker = (
        lax.broadcasted_iota(jnp.int32, (CLIENTS, CLIENTS), 0) == ids_ref[...]
    ).astype(BF16)
    pre_send[...] = dot_tn(picker, cols).reshape(NC, SLOTS, NK * width)
    ld_table.wait()
    tablef[...] = jnp.zeros_like(tablef)
    tablef[0:classes, :] = table[...].astype(F32)
    for s in range(SLOTS):
        for j in range(SAMPLES // 128):
            lab[s : s + 1, j * 128 : (j + 1) * 128] = labels_ref[s * 4 + j : s * 4 + j + 1, :]
    ld_w.wait()

    pl.semaphore_wait(barrier, NE - 1 + NZL - 1 + NC - 1)

    qrow = x * QR + core * (QR // NK)
    qpart = pl.ds(pl.multiple_of(qrow, QR // NK), QR // NK)
    half = HB // NK
    cut = 64

    def hpart(first, last):
        return pl.ds(pl.multiple_of(core * half + first, cut), last - first)

    w_z = remote(wfull.at[zh, y, qpart], wfull.at[zh, y, qpart], wz_s, wz_r, dev(z_=2 * NZL - 1 - z))
    w_z.start()

    def send_pre(d, carry):
        to = (c + d) % NC
        remote(pre_send.at[to], pre_recv.at[c], pre_ssem, pre_rsem, {"client": to}).start()
        return carry

    lax.fori_loop(1, NC, send_pre, 0)
    own_pre = pltpu.make_async_copy(pre_send.at[c], pre_recv.at[c], pre_rsem)
    own_pre.start()
    w_a = []
    for d in range(1, NY):
        part = wfull.at[zh, y, hpart(0, cut)]
        cp = remote(part, part, wa_s.at[0, d - 1], wa_r.at[0, d - 1], dev(y_=(y + d) % NY))
        cp.start()
        w_a.append(cp)

    w_z.wait()
    w_b = []
    for d in range(1, NY):
        part = wfull.at[1 - zh, y, qpart]
        cp = remote(part, part, wb_s.at[d - 1], wb_r.at[d - 1], dev(y_=(y + d) % NY))
        cp.start()
        w_b.append(cp)

    def along_x(i, yy):
        copies = []
        for d in range(1, NX):
            part = wfull.at[1 - zh, yy, qpart]
            cp = remote(part, part, wc_s.at[i, d - 1], wc_r.at[i, d - 1], dev(x_=(x + d) % NX))
            cp.start()
            copies.append(cp)
        return copies

    w_c = [along_x(0, y)]

    pltpu.make_async_copy(pre_recv, pre_recv, pre_rsem).wait()
    for j in range(HID // CPAD):
        pre_own[:, j * CPAD : (j + 1) * CPAD] = pre_recv[NK * j] + pre_recv[NK * j + 1]
    pre = pre_own[...]
    sig = sigmoid(pre)
    spre[...] = pre * sig
    dp = sig * (1.0 + pre * (1.0 - sig))
    for j in range(NE):
        dpre[j] = dp[:, j * HB : (j + 1) * HB]

    live = lax.broadcasted_iota(jnp.int32, (CPAD, HB), 0) < classes

    def emit_codes(i, carry):
        s, h = i // NE, i % NE
        lanes = pl.ds(pl.multiple_of(h * HB, HB), HB)
        within = pl.ds(pl.multiple_of((h // NZH) * HB, HB), HB)
        rows = pl.ds(pl.multiple_of(s * CPAD, CPAD), CPAD)
        v = spre[pl.ds(s, 1), lanes] + tablef[:, lanes]
        g = sigmoid(v)
        a = v * g
        code[h % NZH, rows, within] = jnp.where(live, a, 0.0).astype(BF16)
        dcode[rows, lanes] = (g + a * (1.0 - g)).astype(BF16)
        return carry

    def turn(i, carry):
        s, h = i // NE, i % NE
        rows = pl.ds(pl.multiple_of(s * CPAD, CPAD), CPAD)
        within = pl.ds(pl.multiple_of((h // NZH) * HB, HB), HB)
        code_t[h, :, rows] = code[h % NZH, rows, within].T
        return carry

    lax.fori_loop(0, SLOTS * NE, emit_codes, 0, unroll=2)

    for d in range(1, NY):
        part = wfull.at[zh, y, hpart(cut, half)]
        cp = remote(part, part, wa_s.at[1, d - 1], wa_r.at[1, d - 1], dev(y_=(y + d) % NY))
        cp.start()
        w_a.append(cp)
    for d in range(1, NY):
        w_b[d - 1].wait()
        w_c.append(along_x(d, (y + NY - d) % NY))

    def to_core(i, q):
        part = wfull.at[1 - zh, :, pl.ds(pl.multiple_of(q * QR + core * (QR // NK), QR // NK), QR // NK)]
        return remote(part, part, wd_s.at[i], wd_r.at[i], dev(core_=1 - core))

    w_d = [to_core(3, x)]
    w_d[0].start()

    lax.fori_loop(0, SLOTS * NE // 2, turn, 0)
    trunk_perm[...] = dot_tn(picker, trunk[...]).astype(BF16)

    w_e = []
    for d in range(1, NY):
        w_a[d - 1].wait()
        w_a[NY - 1 + d - 1].wait()
        part = wfull.at[zh, (y + NY - d) % NY, hpart(0, half)]
        cp = remote(part, part, wd_s.at[d - 1], wd_r.at[d - 1], dev(core_=1 - core))
        cp.start()
        w_e.append(cp)
    lax.fori_loop(SLOTS * NE // 2, SLOTS * NE, turn, 0)
    for cp in w_e:
        cp.wait()

    def heads_first(m, carry):
        rows = pl.ds(pl.multiple_of(m * HB, HB), HB)
        hacc[rows, :] = dot(code[zh, rows, :], wfull[zh].reshape(HID // NZH, FEAT))
        return carry

    lax.fori_loop(0, ROWS // HB // 2, heads_first, 0)

    for d in range(1, NX):
        for copies in w_c:
            copies[d - 1].wait()
        cp = to_core(3 + d, (x + NX - d) % NX)
        cp.start()
        w_d.append(cp)
    lax.fori_loop(ROWS // HB // 2, ROWS // HB, heads_first, 0)
    for cp in w_d:
        cp.wait()

    def heads_rest(m, carry):
        rows = pl.ds(pl.multiple_of(m * HB, HB), HB)
        part = dot(code[1 - zh, rows, :], wfull[1 - zh].reshape(HID // NZH, FEAT))
        heads[rows, :] = (hacc[rows, :] + part).astype(BF16)
        return carry

    lax.fori_loop(0, ROWS // HB, heads_rest, 0)
    ld_feats.wait()

    kids = lax.broadcasted_iota(jnp.int32, (CPAD, SAMPLES), 0)
    valid = kids < classes
    kids = kids + e * classes

    def onehot_of(s):
        return jnp.logical_and(kids == lab[pl.ds(s, 1), :], valid)

    def logits_of(s, carry):
        rows = pl.ds(pl.multiple_of(s * CPAD, CPAD), CPAD)
        frows = pl.ds(pl.multiple_of(s * SAMPLES, SAMPLES), SAMPLES)
        lg = dot_nt(heads[rows, :], feats[frows, :])
        top = jnp.max(jnp.where(valid, lg, -jnp.inf), axis=0, keepdims=True)
        ex = jnp.where(valid, jnp.exp(lg - top), 0.0)
        probs[rows, :] = ex
        tops[pl.ds(s, 1), :] = top
        sums[pl.ds(s, 1), :] = jnp.sum(ex, axis=0, keepdims=True)
        tg_send[pl.ds(s, 1), :] = jnp.sum(jnp.where(onehot_of(s), lg, 0.0), axis=0, keepdims=True)
        return carry

    hs = SLOTS // GROUPS

    def st_copies(g):
        return [
            remote(st_send.at[g], st_recv.at[g, d - 1], st_s.at[g, d - 1], st_r.at[g, d - 1], {"emit": (e + d) % NE})
            for d in range(1, NE)
        ]

    st = []
    for g in range(GROUPS):
        lax.fori_loop(g * hs, (g + 1) * hs, logits_of, 0, unroll=2)
        st_send[g] = tops[g * hs : (g + 1) * hs, :] + jnp.log(sums[g * hs : (g + 1) * hs, :])
        st.append(st_copies(g))
        for cp in st[g]:
            cp.start()

    def combine(g):
        for cp in st[g]:
            cp.wait()
        lse = st_send[g]
        gtop = lse
        for d in range(NE - 1):
            gtop = jnp.maximum(gtop, st_recv[g, d])
        total = jnp.exp(lse - gtop)
        for d in range(NE - 1):
            total += jnp.exp(st_recv[g, d] - gtop)
        top = gtop + jnp.log(total)
        part = slice(g * hs, (g + 1) * hs)
        logz[part, :] = top
        sums[part, :] = jnp.exp(tops[part, :] - top)

    def grads_of(s, carry):
        rows = pl.ds(pl.multiple_of(s * CPAD, CPAD), CPAD)
        frows = pl.ds(pl.multiple_of(s * SAMPLES, SAMPLES), SAMPLES)
        g = probs[rows, :] * sums[pl.ds(s, 1), :] - onehot_of(s).astype(F32)
        gh[rows, :] = dot((g * (1.0 / CLIENTS)).astype(BF16), feats[frows, :]).astype(BF16)
        return carry

    for g in range(GROUPS):
        combine(g)
        lax.fori_loop(g * hs, (g + 1) * hs, grads_of, 0, unroll=2)
    tg = []
    for d in range(1, NE):
        cp = remote(tg_send, tg_recv.at[d - 1], res_s.at[d - 1], res_r.at[d - 1], {"emit": (e + d) % NE})
        cp.start()
        tg.append(cp)

    def core_copy(n):
        return remote(eg.at[n, 1 - core], egr.at[n], core_s.at[n], core_r.at[n], dev(core_=1 - core))

    def x1_copy(i, d):
        to = (x + d) % NX
        part = pl.ds(pl.multiple_of(to * 32, 32), 32)
        return remote(am.at[2 * i, part], rx.at[i, d - 1], x1_s.at[i, d - 1], x1_r.at[i, d - 1], dev(x_=to))

    def along_y(i):
        return (y + 1 + 2 * i - 3 * (i // 2)) % NY

    def y1_copy(i):
        return remote(am.at[2 * i + 1], ry.at[i], y1_s.at[i], y1_r.at[i], dev(y_=along_y(i)))

    def compute_chunk(i, half):
        n = 2 * i + half
        part = dot(code_t[along_y(i) * NZH + half], gh[...]).reshape(HB // (NK * 8), NK, 8, FEAT)
        for k in range(NK):
            eg[n, k] = part[:, k].reshape(HB // NK, FEAT).astype(BF16)
        core_copy(n).start()

    def sum_codes(h):
        gc = dot_nt(gh[...], wfull[h % NZH, h // NZH])
        lanes = pl.ds(pl.multiple_of(h * HB, HB), HB)
        for s in range(SLOTS):
            part = gc[s * CPAD : (s + 1) * CPAD] * dcode[s * CPAD : (s + 1) * CPAD, lanes].astype(F32)
            gs_send[h, s : s + 1, :] = jnp.sum(part, axis=0, keepdims=True)

    def pass_on(i, half):
        n = 2 * i + half
        core_copy(n).wait()
        am[n] = (eg[n, core].astype(F32) + egr[n].astype(F32)).astype(BF16)
        if half == 0:
            for d in range(1, NX):
                x1_copy(i, d).start()

    def pass_on_y(i):
        pass_on(i, 1)
        y1_copy(i).start()

    def y2_copy(i):
        return remote(bx.at[i], rxy.at[i], y2_s.at[i], y2_r.at[i], dev(y_=along_y(i)))

    xpart = pl.ds(pl.multiple_of(x * 32, 32), 32)

    def along_x_sum(i):
        for d in range(1, NX):
            x1_copy(i, d).wait()
        acc = am[2 * i, xpart, :].astype(F32)
        for d in range(NX - 1):
            acc += rx[i, d].astype(F32)
        bx[i] = acc.astype(BF16)

    def first_chunks(j, carry):
        compute_chunk(j, 1)
        return carry

    def next_chunks(j, carry):
        compute_chunk(j, 0)
        pass_on_y(j)
        return carry

    def sum_step(h, carry):
        sum_codes(h)
        return carry

    lax.fori_loop(0, NY - 1, first_chunks, 0)
    lax.fori_loop(0, NY - 1, next_chunks, 0)
    compute_chunk(NY - 1, 0)
    pass_on(0, 0)
    compute_chunk(NY - 1, 1)
    pass_on(1, 0)
    sum_codes(0)
    pass_on(2, 0)
    sum_codes(1)
    pass_on(3, 0)
    pass_on(3, 1)
    lax.fori_loop(2, NE, sum_step, 0)

    gs_half[...] = gs_send[...].astype(BF16)
    gs = []
    for d in range(1, NE):
        to = (e + d) % NE
        cp = remote(gs_half.at[to], gs_recv.at[d - 1], gs_s.at[d - 1], gs_r.at[d - 1], {"emit": to})
        cp.start()
        gs.append(cp)

    acc = am[2 * NY - 1].astype(F32)
    for i in range(NY - 1):
        y1_copy(i).wait()
        acc += ry[i].astype(F32)
    by[...] = acc.astype(BF16)
    x2 = []
    for d in range(1, NX):
        to = (x + d) % NX
        part = pl.ds(pl.multiple_of(to * 32, 32), 32)
        cp = remote(by.at[part], ryx.at[d - 1], x2_s.at[d - 1], x2_r.at[d - 1], dev(x_=to))
        cp.start()
        x2.append(cp)
    def second_step(i, carry):
        along_x_sum(i)
        y2_copy(i).start()
        return carry

    lax.fori_loop(0, NY - 1, second_step, 0)

    for cp in gs:
        cp.wait()
    block = gs_send[e]
    for d in range(NE - 1):
        block = block + gs_recv[d].astype(F32)
    gp_send[...] = (block * dpre[e]).astype(BF16)

    def send_gp(d, carry):
        remote(gp_send, gp_recv.at[c], gp_ssem, gp_rsem, {"client": (c + d) % NC}).start()
        return carry

    lax.fori_loop(1, NC, send_gp, 0)
    own_gp = pltpu.make_async_copy(gp_send, gp_recv.at[c], gp_rsem)
    own_gp.start()

    along_x_sum(NY - 1)
    for i in range(NY - 1):
        y2_copy(i).wait()
    acc = bx[NY - 1].astype(F32)
    for d in range(NY - 1):
        acc += rxy[d].astype(F32)
    cz[0:NZL] = acc.astype(BF16).reshape(NZL, 8, FEAT)
    for cp in x2:
        cp.wait()
    acc = by[xpart, :].astype(F32)
    for d in range(NX - 1):
        acc += ryx[d].astype(F32)
    cz[NZL:] = acc.astype(BF16).reshape(NZL, 8, FEAT)
    nz = NZH * NZL
    zs = []
    for d in range(1, nz):
        to = (z + d) % nz
        cp = remote(cz.at[to], rz.at[d - 1], z_s.at[d - 1], z_r.at[d - 1], dev(z_=to))
        cp.start()
        zs.append(cp)

    for cp in tg:
        cp.wait()
    rest = logz[...] - tg_send[...]
    for d in range(NE - 1):
        rest = rest - tg_recv[d]
    for s in range(SLOTS):
        for j in range(SAMPLES // 128):
            loss_ref[s * 4 + j : s * 4 + j + 1, :] = rest[s : s + 1, j * 128 : (j + 1) * 128]

    pltpu.make_async_copy(gp_recv, gp_recv, gp_rsem).wait()
    select = (
        lax.broadcasted_iota(jnp.int32, (8, HB), 1) == lax.broadcasted_iota(jnp.int32, (8, HB), 0) + c * 8
    ).astype(BF16)
    mine = dot_nt(select, gp_recv[...].reshape(CLIENTS, HB)).astype(BF16)
    tgrad_ref[...] = dot(mine, trunk_perm[...])

    for cp in zs:
        cp.wait()
    acc = cz[z].astype(F32)
    for d in range(nz - 1):
        acc += rz[d].astype(F32)
    egrad_ref[...] = acc

    remote(pre_send.at[0 : NC - 1], pre_recv.at[0 : NC - 1], pre_ssem, pre_rsem, {"client": (c + 1) % NC}).wait_send()
    remote(gp_recv.at[0 : NC - 1], gp_recv.at[0 : NC - 1], gp_ssem, gp_rsem, {"client": (c + 1) % NC}).wait_send()


def hand_over(loss_in, egrad_in, tgrad_in, loss_ref, egrad_ref, tgrad_ref):
    loss_ref[...] = loss_in[...]
    egrad_ref[...] = egrad_in[...]
    tgrad_ref[...] = tgrad_in[...]


def per_device(features, labels, client_ids, trunk_in, trunk_weight, class_table, emit_weight):
    vm = pltpu.VMEM
    dma = pltpu.SemaphoreType.DMA
    half = HB // NK
    scratch = [
        vm((SLOTS * SAMPLES, FEAT), BF16), vm((SLOTS, SAMPLES), jnp.int32), vm((CLIENTS, HID), BF16), vm((trunk_weight.shape[1], HID), BF16),
        vm(class_table.shape, BF16), vm((CPAD, HID), F32), vm((NZH, NY, HB, FEAT), BF16),
        vm((NC, SLOTS, CPAD), F32), vm((NC, SLOTS, CPAD), F32), vm((SLOTS, HID), F32), vm((SLOTS, HID), F32),
        vm((NE, SLOTS, HB), F32),
        vm((NZH, ROWS, HID // NZH), BF16), vm((NE, HB, ROWS), BF16), vm((ROWS, HID), BF16), vm((ROWS, FEAT), F32),
        vm((ROWS, FEAT), BF16),
        vm((ROWS, SAMPLES), F32), vm((SLOTS, SAMPLES), F32),
        vm((SLOTS, SAMPLES), F32), vm((SLOTS, SAMPLES), F32),
        vm((GROUPS, SLOTS // GROUPS, SAMPLES), F32), vm((GROUPS, NE - 1, SLOTS // GROUPS, SAMPLES), F32), vm((SLOTS, SAMPLES), F32),
        vm((NE - 1, SLOTS, SAMPLES), F32),
        vm((ROWS, FEAT), BF16), vm((NE, NK, half, FEAT), BF16), vm((NE, half, FEAT), BF16), vm((NE, half, FEAT), BF16),
        vm((NY, NX - 1, 32, FEAT), BF16), vm((NY - 1, half, FEAT), BF16),
        vm((NY, 32, FEAT), BF16), vm((NY - 1, 32, FEAT), BF16), vm((half, FEAT), BF16), vm((NX - 1, 32, FEAT), BF16),
        vm((NZH * NZL, 8, FEAT), BF16), vm((NZH * NZL - 1, 8, FEAT), BF16),
        vm((NE, SLOTS, HB), F32), vm((NE, SLOTS, HB), BF16), vm((NE - 1, SLOTS, HB), BF16), vm((SLOTS, HB), BF16), vm((NC, SLOTS, HB), BF16),
        vm((CLIENTS, HID), BF16),
        dma((5,)), dma, dma,
        dma((2, 3)), dma((2, 3)), dma, dma, dma((3,)), dma((3,)), dma((4, 3)), dma((4, 3)), dma((7,)), dma((7,)),
        dma((GROUPS, 7)), dma((GROUPS, 7)), dma((7,)), dma((7,)), dma((8,)), dma((8,)),
        dma((4, 3)), dma((4, 3)), dma((3,)), dma((3,)), dma((3,)), dma((3,)), dma((3,)), dma((3,)), dma((7,)), dma((7,)),
        dma((7,)), dma((7,)), dma, dma,
    ]
    hbm = pl.BlockSpec(memory_space=pl.ANY)
    here = pl.BlockSpec(memory_space=pltpu.VMEM)
    loss, egrad, tgrad = pl.pallas_call(
        step_kernel,
        name="hyper_step",
        out_shape=(
            jax.ShapeDtypeStruct((SLOTS * SAMPLES // 128, 128), F32),
            jax.ShapeDtypeStruct((HID // (NE * NC), FEAT), F32),
            jax.ShapeDtypeStruct((HID // (NE * NC), HID), F32),
        ),
        in_specs=[hbm, here, here, hbm, hbm, hbm, hbm],
        out_specs=(here, here, here),
        scratch_shapes=scratch,
        compiler_params=pltpu.CompilerParams(collective_id=0, has_side_effects=True, vmem_limit_bytes=56 << 20),
    )(
        features, labels.reshape(SLOTS * SAMPLES // 128, 128), client_ids.reshape(1, CLIENTS), trunk_in, trunk_weight.T,
        class_table, emit_weight,
    )
    outs = (loss, egrad, tgrad)
    loss, egrad, tgrad = pl.pallas_call(
        hand_over,
        name="hand_over",
        out_shape=tuple(jax.ShapeDtypeStruct(o.shape, o.dtype) for o in outs),
        in_specs=[here] * 3,
        out_specs=(here,) * 3,
    )(*outs)
    return loss.reshape(SLOTS * SAMPLES), egrad, tgrad.T


def solution(mesh):
    return jax.shard_map(
        per_device,
        mesh=mesh,
        in_specs=(
            P("client", None),
            P("client"),
            P(),
            P(),
            P(None, "client"),
            P("emit", None),
            P("emit", None),
        ),
        out_specs=(P("client"), P(("emit", "client"), None), P(None, ("emit", "client"))),
        check_vma=False,
    )
```

```python
import jax
import jax.numpy as jnp
from jax import lax
from jax.experimental import pallas as pl
from jax.experimental.pallas import tpu as pltpu
from jax.sharding import PartitionSpec as P

MESH = pl.DeviceIdType.MESH
BF16 = jnp.bfloat16
F32 = jnp.float32

NY, NZH, NX, NZL, NK = 4, 2, 4, 4, 2
NE, NC = NY * NZH, NX * NZL * NK
SLOTS = 8
SAMPLES = 512
GROUPS = 4
CPAD = 128
ROWS = SLOTS * CPAD
HID = 2048
FEAT = 768
CLIENTS = 256
HB = HID // NE
QR = HB // NX


def dot(a, b):
    return jnp.dot(a, b, preferred_element_type=F32)


def dot_nt(a, b):
    return lax.dot_general(a, b, (((1,), (1,)), ((), ())), preferred_element_type=F32)


def dot_tn(a, b):
    return lax.dot_general(a, b, (((0,), (0,)), ((), ())), preferred_element_type=F32)


def sigmoid(v):
    return 0.5 * jnp.tanh(0.5 * v) + 0.5


def step_kernel(
    feats_hbm, labels_ref, ids_ref, trunk_hbm, tw_hbm, table_hbm, emit_hbm,
    loss_ref, egrad_ref, tgrad_ref,
    feats, lab, trunk, tw, table, tablef, wfull,
    pre_send, pre_recv, pre_own, spre, dpre,
    code, code_t, dcode, hacc, heads, probs, tops,
    sums, logz, st_send, st_recv, tg_send, tg_recv,
    gh, eg, egr, am, rx, ry, bx, rxy, by, ryx, cz, rz,
    gs_send, gs_half, gs_recv, gp_send, gp_recv, trunk_perm,
    loc_sem, pre_ssem, pre_rsem,
    wa_s, wa_r, wz_s, wz_r, wb_s, wb_r, wc_s, wc_r, wd_s, wd_r,
    st_s, st_r, res_s, res_r, core_s, core_r,
    x1_s, x1_r, y1_s, y1_r, x2_s, x2_r, y2_s, y2_r, z_s, z_r,
    gs_s, gs_r, gp_ssem, gp_rsem,
):
    e = lax.axis_index("emit")
    c = lax.axis_index("client")
    y, zh = e // NZH, e % NZH
    x, zl, core = c // (NZL * NK), (c // NK) % NZL, c % NK
    z = zh * NZL + zl
    classes = table_hbm.shape[0]

    def dev(y_=None, z_=None, x_=None, core_=None):
        y_ = y if y_ is None else y_
        z_ = z if z_ is None else z_
        x_ = x if x_ is None else x_
        core_ = core if core_ is None else core_
        return {"emit": y_ * NZH + z_ // NZL, "client": (x_ * NZL + z_ % NZL) * NK + core_}

    def remote(src, dst, ssem, rsem, to):
        return pltpu.make_async_remote_copy(
            src_ref=src, dst_ref=dst, send_sem=ssem, recv_sem=rsem, device_id=to, device_id_type=MESH
        )

    barrier = pltpu.get_barrier_semaphore()

    def greet(to):
        pl.semaphore_signal(barrier, inc=1, device_id=to, device_id_type=MESH)

    def greet_client(d, carry):
        greet({"client": (c + d) % NC})
        return carry

    for d in range(1, NE):
        greet({"emit": (e + d) % NE})
    for d in range(1, NZL):
        greet(dev(z_=(1 - zh) * NZL + (zl + d) % NZL))
    lax.fori_loop(1, NC, greet_client, 0)

    ld_trunk = pltpu.make_async_copy(trunk_hbm, trunk, loc_sem.at[0])
    ld_tw = pltpu.make_async_copy(tw_hbm, tw, loc_sem.at[1])
    ld_w = pltpu.make_async_copy(emit_hbm, wfull.at[zh, y], loc_sem.at[2])
    ld_table = pltpu.make_async_copy(table_hbm, table, loc_sem.at[3])
    ld_feats = pltpu.make_async_copy(feats_hbm, feats, loc_sem.at[4])
    for cp in (ld_trunk, ld_tw, ld_w, ld_table, ld_feats):
        cp.start()

    ld_trunk.wait()
    ld_tw.wait()
    cols = dot_nt(trunk[...], tw[...]).astype(BF16)
    width = cols.shape[1]
    spread = (
        lax.broadcasted_iota(jnp.int32, (width, NK * width), 1)
        == lax.broadcasted_iota(jnp.int32, (width, NK * width), 0) + core * width
    ).astype(BF16)
    cols = dot(cols, spread).astype(BF16)
    picker = (
        lax.broadcasted_iota(jnp.int32, (CLIENTS, CLIENTS), 0) == ids_ref[...]
    ).astype(BF16)
    pre_send[...] = dot_tn(picker, cols).reshape(NC, SLOTS, NK * width)
    ld_table.wait()
    tablef[...] = jnp.zeros_like(tablef)
    tablef[0:classes, :] = table[...].astype(F32)
    for s in range(SLOTS):
        for j in range(SAMPLES // 128):
            lab[s : s + 1, j * 128 : (j + 1) * 128] = labels_ref[s * 4 + j : s * 4 + j + 1, :]
    ld_w.wait()

    pl.semaphore_wait(barrier, NE - 1 + NZL - 1 + NC - 1)

    qrow = x * QR + core * (QR // NK)
    qpart = pl.ds(pl.multiple_of(qrow, QR // NK), QR // NK)
    half = HB // NK
    cut = 64

    def hpart(first, last):
        return pl.ds(pl.multiple_of(core * half + first, cut), last - first)

    w_z = remote(wfull.at[zh, y, qpart], wfull.at[zh, y, qpart], wz_s, wz_r, dev(z_=2 * NZL - 1 - z))
    w_z.start()

    def send_pre(d, carry):
        to = (c + d) % NC
        remote(pre_send.at[to], pre_recv.at[c], pre_ssem, pre_rsem, {"client": to}).start()
        return carry

    lax.fori_loop(1, NC, send_pre, 0)
    own_pre = pltpu.make_async_copy(pre_send.at[c], pre_recv.at[c], pre_rsem)
    own_pre.start()
    w_a = []
    for d in range(1, NY):
        part = wfull.at[zh, y, hpart(0, cut)]
        cp = remote(part, part, wa_s.at[0, d - 1], wa_r.at[0, d - 1], dev(y_=(y + d) % NY))
        cp.start()
        w_a.append(cp)

    w_z.wait()
    w_b = []
    for d in range(1, NY):
        part = wfull.at[1 - zh, y, qpart]
        cp = remote(part, part, wb_s.at[d - 1], wb_r.at[d - 1], dev(y_=(y + d) % NY))
        cp.start()
        w_b.append(cp)

    def along_x(i, yy):
        copies = []
        for d in range(1, NX):
            part = wfull.at[1 - zh, yy, qpart]
            cp = remote(part, part, wc_s.at[i, d - 1], wc_r.at[i, d - 1], dev(x_=(x + d) % NX))
            cp.start()
            copies.append(cp)
        return copies

    w_c = [along_x(0, y)]

    pltpu.make_async_copy(pre_recv, pre_recv, pre_rsem).wait()
    for j in range(HID // CPAD):
        pre_own[:, j * CPAD : (j + 1) * CPAD] = pre_recv[NK * j] + pre_recv[NK * j + 1]
    pre = pre_own[...]
    sig = sigmoid(pre)
    spre[...] = pre * sig
    dp = sig * (1.0 + pre * (1.0 - sig))
    for j in range(NE):
        dpre[j] = dp[:, j * HB : (j + 1) * HB]

    live = lax.broadcasted_iota(jnp.int32, (CPAD, HB), 0) < classes

    def emit_codes(i, carry):
        s, h = i // NE, i % NE
        lanes = pl.ds(pl.multiple_of(h * HB, HB), HB)
        within = pl.ds(pl.multiple_of((h // NZH) * HB, HB), HB)
        rows = pl.ds(pl.multiple_of(s * CPAD, CPAD), CPAD)
        v = spre[pl.ds(s, 1), lanes] + tablef[:, lanes]
        g = sigmoid(v)
        a = v * g
        code[h % NZH, rows, within] = jnp.where(live, a, 0.0).astype(BF16)
        dcode[rows, lanes] = (g + a * (1.0 - g)).astype(BF16)
        return carry

    def turn(i, carry):
        s, h = i // NE, i % NE
        rows = pl.ds(pl.multiple_of(s * CPAD, CPAD), CPAD)
        within = pl.ds(pl.multiple_of((h // NZH) * HB, HB), HB)
        code_t[h, :, rows] = code[h % NZH, rows, within].T
        return carry

    lax.fori_loop(0, SLOTS * NE, emit_codes, 0, unroll=2)

    for d in range(1, NY):
        part = wfull.at[zh, y, hpart(cut, half)]
        cp = remote(part, part, wa_s.at[1, d - 1], wa_r.at[1, d - 1], dev(y_=(y + d) % NY))
        cp.start()
        w_a.append(cp)
    for d in range(1, NY):
        w_b[d - 1].wait()
        w_c.append(along_x(d, (y + NY - d) % NY))

    def to_core(i, q):
        part = wfull.at[1 - zh, :, pl.ds(pl.multiple_of(q * QR + core * (QR // NK), QR // NK), QR // NK)]
        return remote(part, part, wd_s.at[i], wd_r.at[i], dev(core_=1 - core))

    w_d = [to_core(3, x)]
    w_d[0].start()

    lax.fori_loop(0, SLOTS * NE // 2, turn, 0)
    trunk_perm[...] = dot_tn(picker, trunk[...]).astype(BF16)

    w_e = []
    for d in range(1, NY):
        w_a[d - 1].wait()
        w_a[NY - 1 + d - 1].wait()
        part = wfull.at[zh, (y + NY - d) % NY, hpart(0, half)]
        cp = remote(part, part, wd_s.at[d - 1], wd_r.at[d - 1], dev(core_=1 - core))
        cp.start()
        w_e.append(cp)
    lax.fori_loop(SLOTS * NE // 2, SLOTS * NE, turn, 0)
    for cp in w_e:
        cp.wait()

    def heads_first(m, carry):
        rows = pl.ds(pl.multiple_of(m * 2 * HB, 2 * HB), 2 * HB)
        hacc[rows, :] = dot(code[zh, rows, :], wfull[zh].reshape(HID // NZH, FEAT))
        return carry

    lax.fori_loop(0, ROWS // HB // 4, heads_first, 0)

    for d in range(1, NX):
        for copies in w_c:
            copies[d - 1].wait()
        cp = to_core(3 + d, (x + NX - d) % NX)
        cp.start()
        w_d.append(cp)
    lax.fori_loop(ROWS // HB // 4, ROWS // HB // 2, heads_first, 0)
    for cp in w_d:
        cp.wait()

    def heads_rest(m, carry):
        rows = pl.ds(pl.multiple_of(m * 2 * HB, 2 * HB), 2 * HB)
        part = dot(code[1 - zh, rows, :], wfull[1 - zh].reshape(HID // NZH, FEAT))
        heads[rows, :] = (hacc[rows, :] + part).astype(BF16)
        return carry

    lax.fori_loop(0, ROWS // HB // 2, heads_rest, 0)
    ld_feats.wait()

    kids = lax.broadcasted_iota(jnp.int32, (CPAD, SAMPLES), 0)
    valid = kids < classes
    kids = kids + e * classes

    def onehot_of(s):
        return jnp.logical_and(kids == lab[pl.ds(s, 1), :], valid)

    def logits_of(s, carry):
        rows = pl.ds(pl.multiple_of(s * CPAD, CPAD), CPAD)
        frows = pl.ds(pl.multiple_of(s * SAMPLES, SAMPLES), SAMPLES)
        lg = dot_nt(heads[rows, :], feats[frows, :])
        top = jnp.max(jnp.where(valid, lg, -jnp.inf), axis=0, keepdims=True)
        ex = jnp.where(valid, jnp.exp(lg - top), 0.0)
        probs[rows, :] = ex
        tops[pl.ds(s, 1), :] = top
        sums[pl.ds(s, 1), :] = jnp.sum(ex, axis=0, keepdims=True)
        tg_send[pl.ds(s, 1), :] = jnp.sum(jnp.where(onehot_of(s), lg, 0.0), axis=0, keepdims=True)
        return carry

    hs = SLOTS // GROUPS

    def st_copies(g):
        return [
            remote(st_send.at[g], st_recv.at[g, d - 1], st_s.at[g, d - 1], st_r.at[g, d - 1], {"emit": (e + d) % NE})
            for d in range(1, NE)
        ]

    st = []
    for g in range(GROUPS):
        lax.fori_loop(g * hs, (g + 1) * hs, logits_of, 0, unroll=2)
        st_send[g] = tops[g * hs : (g + 1) * hs, :] + jnp.log(sums[g * hs : (g + 1) * hs, :])
        st.append(st_copies(g))
        for cp in st[g]:
            cp.start()

    def combine(g):
        for cp in st[g]:
            cp.wait()
        lse = st_send[g]
        gtop = lse
        for d in range(NE - 1):
            gtop = jnp.maximum(gtop, st_recv[g, d])
        total = jnp.exp(lse - gtop)
        for d in range(NE - 1):
            total += jnp.exp(st_recv[g, d] - gtop)
        top = gtop + jnp.log(total)
        part = slice(g * hs, (g + 1) * hs)
        logz[part, :] = top
        sums[part, :] = jnp.exp(tops[part, :] - top)

    def grads_of(s, carry):
        rows = pl.ds(pl.multiple_of(s * CPAD, CPAD), CPAD)
        frows = pl.ds(pl.multiple_of(s * SAMPLES, SAMPLES), SAMPLES)
        g = probs[rows, :] * sums[pl.ds(s, 1), :] - onehot_of(s).astype(F32)
        gh[rows, :] = dot((g * (1.0 / CLIENTS)).astype(BF16), feats[frows, :]).astype(BF16)
        return carry

    for g in range(GROUPS):
        combine(g)
        lax.fori_loop(g * hs, (g + 1) * hs, grads_of, 0, unroll=2)
    tg = []
    for d in range(1, NE):
        cp = remote(tg_send, tg_recv.at[d - 1], res_s.at[d - 1], res_r.at[d - 1], {"emit": (e + d) % NE})
        cp.start()
        tg.append(cp)

    def core_copy(n):
        return remote(eg.at[n, 1 - core], egr.at[n], core_s.at[n], core_r.at[n], dev(core_=1 - core))

    def x1_copy(i, d):
        to = (x + d) % NX
        part = pl.ds(pl.multiple_of(to * 32, 32), 32)
        return remote(am.at[2 * i, part], rx.at[i, d - 1], x1_s.at[i, d - 1], x1_r.at[i, d - 1], dev(x_=to))

    def along_y(i):
        return (y + 1 + 2 * i - 3 * (i // 2)) % NY

    def y1_copy(i):
        return remote(am.at[2 * i + 1], ry.at[i], y1_s.at[i], y1_r.at[i], dev(y_=along_y(i)))

    def compute_chunk(i, half):
        n = 2 * i + half
        part = dot(code_t[along_y(i) * NZH + half], gh[...]).reshape(HB // (NK * 8), NK, 8, FEAT)
        for k in range(NK):
            eg[n, k] = part[:, k].reshape(HB // NK, FEAT).astype(BF16)
        core_copy(n).start()

    def sum_codes(h):
        gc = dot_nt(gh[...], wfull[h % NZH, h // NZH])
        lanes = pl.ds(pl.multiple_of(h * HB, HB), HB)
        for s in range(SLOTS):
            part = gc[s * CPAD : (s + 1) * CPAD] * dcode[s * CPAD : (s + 1) * CPAD, lanes].astype(F32)
            gs_send[h, s : s + 1, :] = jnp.sum(part, axis=0, keepdims=True)

    def pass_on(i, half):
        n = 2 * i + half
        core_copy(n).wait()
        am[n] = (eg[n, core].astype(F32) + egr[n].astype(F32)).astype(BF16)
        if half == 0:
            for d in range(1, NX):
                x1_copy(i, d).start()

    def pass_on_y(i):
        pass_on(i, 1)
        y1_copy(i).start()

    def y2_copy(i):
        return remote(bx.at[i], rxy.at[i], y2_s.at[i], y2_r.at[i], dev(y_=along_y(i)))

    xpart = pl.ds(pl.multiple_of(x * 32, 32), 32)

    def along_x_sum(i):
        for d in range(1, NX):
            x1_copy(i, d).wait()
        acc = am[2 * i, xpart, :].astype(F32)
        for d in range(NX - 1):
            acc += rx[i, d].astype(F32)
        bx[i] = acc.astype(BF16)

    def first_chunks(j, carry):
        compute_chunk(j, 1)
        return carry

    def next_chunks(j, carry):
        compute_chunk(j, 0)
        pass_on_y(j)
        return carry

    def sum_step(h, carry):
        sum_codes(h)
        return carry

    lax.fori_loop(0, NY - 1, first_chunks, 0)
    lax.fori_loop(0, NY - 1, next_chunks, 0)
    compute_chunk(NY - 1, 0)
    pass_on(0, 0)
    compute_chunk(NY - 1, 1)
    pass_on(1, 0)
    sum_codes(0)
    pass_on(2, 0)
    sum_codes(1)
    pass_on(3, 0)
    pass_on(3, 1)
    lax.fori_loop(2, NE, sum_step, 0)

    gs_half[...] = gs_send[...].astype(BF16)
    gs = []
    for d in range(1, NE):
        to = (e + d) % NE
        cp = remote(gs_half.at[to], gs_recv.at[d - 1], gs_s.at[d - 1], gs_r.at[d - 1], {"emit": to})
        cp.start()
        gs.append(cp)

    acc = am[2 * NY - 1].astype(F32)
    for i in range(NY - 1):
        y1_copy(i).wait()
        acc += ry[i].astype(F32)
    by[...] = acc.astype(BF16)
    x2 = []
    for d in range(1, NX):
        to = (x + d) % NX
        part = pl.ds(pl.multiple_of(to * 32, 32), 32)
        cp = remote(by.at[part], ryx.at[d - 1], x2_s.at[d - 1], x2_r.at[d - 1], dev(x_=to))
        cp.start()
        x2.append(cp)
    def second_step(i, carry):
        along_x_sum(i)
        y2_copy(i).start()
        return carry

    lax.fori_loop(0, NY - 1, second_step, 0)

    for cp in gs:
        cp.wait()
    block = gs_send[e]
    for d in range(NE - 1):
        block = block + gs_recv[d].astype(F32)
    gp_send[...] = (block * dpre[e]).astype(BF16)

    def send_gp(d, carry):
        remote(gp_send, gp_recv.at[c], gp_ssem, gp_rsem, {"client": (c + d) % NC}).start()
        return carry

    lax.fori_loop(1, NC, send_gp, 0)
    own_gp = pltpu.make_async_copy(gp_send, gp_recv.at[c], gp_rsem)
    own_gp.start()

    along_x_sum(NY - 1)
    for i in range(NY - 1):
        y2_copy(i).wait()
    acc = bx[NY - 1].astype(F32)
    for d in range(NY - 1):
        acc += rxy[d].astype(F32)
    cz[0:NZL] = acc.astype(BF16).reshape(NZL, 8, FEAT)
    for cp in x2:
        cp.wait()
    acc = by[xpart, :].astype(F32)
    for d in range(NX - 1):
        acc += ryx[d].astype(F32)
    cz[NZL:] = acc.astype(BF16).reshape(NZL, 8, FEAT)
    nz = NZH * NZL
    zs = []
    for d in range(1, nz):
        to = (z + d) % nz
        cp = remote(cz.at[to], rz.at[d - 1], z_s.at[d - 1], z_r.at[d - 1], dev(z_=to))
        cp.start()
        zs.append(cp)

    for cp in tg:
        cp.wait()
    rest = logz[...] - tg_send[...]
    for d in range(NE - 1):
        rest = rest - tg_recv[d]
    for s in range(SLOTS):
        for j in range(SAMPLES // 128):
            loss_ref[s * 4 + j : s * 4 + j + 1, :] = rest[s : s + 1, j * 128 : (j + 1) * 128]

    pltpu.make_async_copy(gp_recv, gp_recv, gp_rsem).wait()
    select = (
        lax.broadcasted_iota(jnp.int32, (8, HB), 1) == lax.broadcasted_iota(jnp.int32, (8, HB), 0) + c * 8
    ).astype(BF16)
    mine = dot_nt(select, gp_recv[...].reshape(CLIENTS, HB)).astype(BF16)
    tgrad_ref[...] = dot(mine, trunk_perm[...])

    for cp in zs:
        cp.wait()
    acc = cz[z].astype(F32)
    for d in range(nz - 1):
        acc += rz[d].astype(F32)
    egrad_ref[...] = acc

    remote(pre_send.at[0 : NC - 1], pre_recv.at[0 : NC - 1], pre_ssem, pre_rsem, {"client": (c + 1) % NC}).wait_send()
    remote(gp_recv.at[0 : NC - 1], gp_recv.at[0 : NC - 1], gp_ssem, gp_rsem, {"client": (c + 1) % NC}).wait_send()


def hand_over(loss_in, egrad_in, tgrad_in, loss_ref, egrad_ref, tgrad_ref):
    loss_ref[...] = loss_in[...]
    egrad_ref[...] = egrad_in[...]
    tgrad_ref[...] = tgrad_in[...]


def per_device(features, labels, client_ids, trunk_in, trunk_weight, class_table, emit_weight):
    vm = pltpu.VMEM
    dma = pltpu.SemaphoreType.DMA
    half = HB // NK
    scratch = [
        vm((SLOTS * SAMPLES, FEAT), BF16), vm((SLOTS, SAMPLES), jnp.int32), vm((CLIENTS, HID), BF16), vm((trunk_weight.shape[1], HID), BF16),
        vm(class_table.shape, BF16), vm((CPAD, HID), F32), vm((NZH, NY, HB, FEAT), BF16),
        vm((NC, SLOTS, CPAD), F32), vm((NC, SLOTS, CPAD), F32), vm((SLOTS, HID), F32), vm((SLOTS, HID), F32),
        vm((NE, SLOTS, HB), F32),
        vm((NZH, ROWS, HID // NZH), BF16), vm((NE, HB, ROWS), BF16), vm((ROWS, HID), BF16), vm((ROWS, FEAT), F32),
        vm((ROWS, FEAT), BF16),
        vm((ROWS, SAMPLES), F32), vm((SLOTS, SAMPLES), F32),
        vm((SLOTS, SAMPLES), F32), vm((SLOTS, SAMPLES), F32),
        vm((GROUPS, SLOTS // GROUPS, SAMPLES), F32), vm((GROUPS, NE - 1, SLOTS // GROUPS, SAMPLES), F32), vm((SLOTS, SAMPLES), F32),
        vm((NE - 1, SLOTS, SAMPLES), F32),
        vm((ROWS, FEAT), BF16), vm((NE, NK, half, FEAT), BF16), vm((NE, half, FEAT), BF16), vm((NE, half, FEAT), BF16),
        vm((NY, NX - 1, 32, FEAT), BF16), vm((NY - 1, half, FEAT), BF16),
        vm((NY, 32, FEAT), BF16), vm((NY - 1, 32, FEAT), BF16), vm((half, FEAT), BF16), vm((NX - 1, 32, FEAT), BF16),
        vm((NZH * NZL, 8, FEAT), BF16), vm((NZH * NZL - 1, 8, FEAT), BF16),
        vm((NE, SLOTS, HB), F32), vm((NE, SLOTS, HB), BF16), vm((NE - 1, SLOTS, HB), BF16), vm((SLOTS, HB), BF16), vm((NC, SLOTS, HB), BF16),
        vm((CLIENTS, HID), BF16),
        dma((5,)), dma, dma,
        dma((2, 3)), dma((2, 3)), dma, dma, dma((3,)), dma((3,)), dma((4, 3)), dma((4, 3)), dma((7,)), dma((7,)),
        dma((GROUPS, 7)), dma((GROUPS, 7)), dma((7,)), dma((7,)), dma((8,)), dma((8,)),
        dma((4, 3)), dma((4, 3)), dma((3,)), dma((3,)), dma((3,)), dma((3,)), dma((3,)), dma((3,)), dma((7,)), dma((7,)),
        dma((7,)), dma((7,)), dma, dma,
    ]
    hbm = pl.BlockSpec(memory_space=pl.ANY)
    here = pl.BlockSpec(memory_space=pltpu.VMEM)
    loss, egrad, tgrad = pl.pallas_call(
        step_kernel,
        name="hyper_step",
        out_shape=(
            jax.ShapeDtypeStruct((SLOTS * SAMPLES // 128, 128), F32),
            jax.ShapeDtypeStruct((HID // (NE * NC), FEAT), F32),
            jax.ShapeDtypeStruct((HID // (NE * NC), HID), F32),
        ),
        in_specs=[hbm, here, here, hbm, hbm, hbm, hbm],
        out_specs=(here, here, here),
        scratch_shapes=scratch,
        compiler_params=pltpu.CompilerParams(collective_id=0, has_side_effects=True, vmem_limit_bytes=56 << 20),
    )(
        features, labels.reshape(SLOTS * SAMPLES // 128, 128), client_ids.reshape(1, CLIENTS), trunk_in, trunk_weight.T,
        class_table, emit_weight,
    )
    outs = (loss, egrad, tgrad)
    loss, egrad, tgrad = pl.pallas_call(
        hand_over,
        name="hand_over",
        out_shape=tuple(jax.ShapeDtypeStruct(o.shape, o.dtype) for o in outs),
        in_specs=[here] * 3,
        out_specs=(here,) * 3,
    )(*outs)
    return loss.reshape(SLOTS * SAMPLES), egrad, tgrad.T


def solution(mesh):
    return jax.shard_map(
        per_device,
        mesh=mesh,
        in_specs=(
            P("client", None),
            P("client"),
            P(),
            P(),
            P(None, "client"),
            P("emit", None),
            P("emit", None),
        ),
        out_specs=(P("client"), P(("emit", "client"), None), P(None, ("emit", "client"))),
        check_vma=False,
    )
```
